32 devices in a mesh: ka: 2 (over core), pair: 16 (over z, y, x).
Axes of the slice: x: 2, y: 2, z: 4, core: 2. Of those that a mesh axis runs over, the one named last changes fastest.
Arguments:
- cond_orbitals: bfloat16 [2, 2048, 2048], P('ka', 'pair'), may hold values from -6 to 6
- cond_energy: float32 [2, 2048], P('ka', 'pair'), may hold values from 0.5 to 8
- val_orbitals: bfloat16 [32, 2048], P(('ka', 'pair')), may hold values from -6 to 6
- val_energy: bfloat16 [32], P(('ka', 'pair')), may hold values from -8 to -0.5
- val_slots: int32 [2, 16, 16], P('ka', 'pair'), may hold values from 0 to 31
- owner_count: int32 [2, 16], P('ka', 'pair'), may hold values from 1 to 16, as said below
Outputs:
- response: float32 [2, 2048, 512], P('ka', 'pair')
The draws below stay inside these ranges and needn't reach their ends.
Inputs may be any that keep to these rules, and one draw needn't show every extreme that they name: `owner_count`: in every lane some owner has exactly 16 live slots.
All inputs are finite; a program needn't handle non-finite values.
Results may differ from the reference program's by a relative error of at most 0.0047.
The reference program's roundings to bfloat16 on the way count: a program that leaves them out, or rounds other values in their place, can miss the bound.
Values may be sent and summed in bfloat16 or wider, within the bound.
A program may use at most 64 MiB of HBM per device.

```python
import jax
import jax.numpy as jnp
from jax import lax

BC = 128
GA = 16
GB = 128
WIN = 512
SLOTS = 16
GRID = 2048
NC = 2048
NVAL = 32
LANES = 2
N_PAIR = 16


def draw_owner_count(key, part):
    first, second = jax.random.split(key)
    counts = jax.random.randint(first, (LANES, N_PAIR), 1, SLOTS + 1)
    where_full = jax.random.randint(second, (LANES, 1), 0, N_PAIR)
    owners = jnp.arange(N_PAIR, dtype=jnp.int32)[None, :]
    return jnp.where(owners == where_full, SLOTS, counts).astype(jnp.int32)


def touch_ends(array, key, least, largest):
    dims = array.shape
    index_at = [jax.random.randint(jax.random.fold_in(key, axis), (), 0, dims[axis]) for axis in range(len(dims))]
    array = array.at[tuple(index_at)].set(least)
    longest = dims.index(max(dims))
    index_at[longest] = (index_at[longest] + 1) % dims[longest]
    return array.at[tuple(index_at)].set(largest)


def block_scale(key, extent, pieces, smallest, largest):
    level = 1.0
    for position, parts in pieces:
        steps = jax.random.uniform(jax.random.fold_in(jax.random.fold_in(key, 6), position), (parts,), jnp.float32, smallest / len(pieces), largest / len(pieces))
        level = level * jnp.repeat(jnp.exp(steps), extent[position] // parts).reshape((-1,) + (1,) * (len(extent) - 1 - position))
    return level


def normal_values(rng, dims, scale, most, cuts=(), kind=jnp.bfloat16):
    values = jax.random.normal(rng, dims, jnp.float32) * scale
    if len(cuts) > 0:
        values = block_scale(rng, dims, cuts, -0.22, 0.18) * values
    return jnp.clip(values, min=-most, max=most).astype(kind)


def setup_inputs(seed: int = 0) -> dict:
    seeds = jax.random.split(jax.random.key(seed), 7)
    return {
        "cond_orbitals": normal_values(seeds[0], (LANES, GRID, NC), 1.0, 6.0, ((0, 2), (1, 16))),
        "cond_energy": jnp.clip(0.5 + 7.5 * jax.random.uniform(seeds[1], (LANES, NC), jnp.float32) ** block_scale(seeds[1], (LANES, NC), ((0, 2), (1, 16)), -0.2, 0.2), 0.5, 8.0),
        "val_orbitals": normal_values(seeds[2], (NVAL, GRID), 1.0, 6.0, ((0, 32),)),
        "val_energy": jnp.clip(-8.0 + 7.5 * jax.random.uniform(seeds[3], (NVAL,), jnp.float32) ** block_scale(seeds[3], (NVAL,), ((0, 32),), -0.2, 0.2), -8.0, -0.5).astype(jnp.bfloat16),
        "val_slots": touch_ends(jax.random.randint(seeds[4], (LANES, N_PAIR, SLOTS), 0, NVAL), jax.random.fold_in(seeds[4], 1), 0, NVAL - 1).astype(jnp.int32),
        "owner_count": draw_owner_count(jax.random.fold_in(seeds[6], 71), 0),
    }


def cosine_table(length):
    freq = lax.iota(jnp.float32, length)[:, None]
    point = lax.iota(jnp.float32, length)[None, :]
    factor = jnp.where(freq == 0, jnp.sqrt(1.0 / length), jnp.sqrt(2.0 / length))
    return (factor * jnp.cos(jnp.pi * (point + 0.5) * freq / length)).astype(jnp.bfloat16)

def owner_terms(picked, e_pick, live, cond_block, e_cond, table_a, table_b):
    slots = picked.shape[0]
    pair_real = (picked[:, None, :].astype(jnp.float32) * cond_block[None].astype(jnp.float32)).astype(jnp.bfloat16)
    count = slots * cond_block.shape[0]
    rows = pair_real.reshape(count * GA, GB)
    first = jnp.dot(rows, table_b.T, preferred_element_type=jnp.float32).astype(jnp.bfloat16)
    first = first.reshape(count, GA, GB)
    moved = jnp.einsum('ja,pak->pjk', table_a.astype(jnp.float32), first.astype(jnp.float32))
    moved = moved.astype(jnp.bfloat16).reshape(count, GA * GB)
    weight = live[:, None] * 2.0 / (e_cond[None, :] - e_pick[:, None])
    weighted = (moved[:, :WIN].astype(jnp.float32) * weight.reshape(count, 1)).astype(jnp.bfloat16)
    return (moved, weighted)

def reference(cond_orbitals, cond_energy, val_orbitals, val_energy, val_slots, owner_count):
    table_a = cosine_table(GA)
    table_b = cosine_table(GB)
    val_float = val_energy.astype(jnp.float32)

    def one_lane(lane):
        cond_all = cond_orbitals[lane].T.reshape(N_PAIR, BC, GA * GB)
        energy_all = cond_energy[lane].reshape(N_PAIR, BC)

        def add_owner(total, owner):
            slots = val_slots[lane, owner]
            picked = jnp.take(val_orbitals, slots, axis=0)
            e_pick = jnp.take(val_float, slots)
            live = (lax.iota(jnp.int32, SLOTS) < owner_count[lane, owner]).astype(jnp.float32)
            moved, weighted = owner_terms(picked, e_pick, live, cond_all[owner], energy_all[owner], table_a, table_b)
            term = lax.dot_general(moved.astype(jnp.float32), weighted.astype(jnp.float32), (((0,), (0,)), ((), ())))
            return (total + term, None)
        start = jnp.zeros((GA * GB, WIN), jnp.float32)
        total, unused = lax.scan(add_owner, start, jnp.arange(N_PAIR, dtype=jnp.int32))
        return total * (2.0 / (SLOTS * BC * N_PAIR))
    return lax.map(one_lane, jnp.arange(LANES, dtype=jnp.int32))
```

```python
import functools

import jax
import jax.numpy as jnp
import numpy as np
from jax import lax
from jax.experimental import pallas as pl
from jax.experimental.pallas import tpu as pltpu
from jax.sharding import PartitionSpec as P

GA = 16
GB = 128
KG = 8
UNROLL_A = 4
LAGS = (1, 3, 4)
MESH = pl.DeviceIdType.MESH
F32 = jnp.float32
BF16 = jnp.bfloat16


def cosine_table(length):
    freq = np.arange(length, dtype=np.float32)[:, None]
    point = np.arange(length, dtype=np.float32)[None, :]
    factor = np.where(freq == 0, np.sqrt(np.float32(1.0 / length)), np.sqrt(np.float32(2.0 / length)))
    angle = np.float32(np.pi) * (point + np.float32(0.5)) * freq / np.float32(length)
    return (factor * np.cos(angle)).astype(jnp.bfloat16)


def xor(value, other, limit):
    out, bit = 0, 1
    while bit < limit:
        out = out + lax.rem(value // bit + other // bit, 2) * bit
        bit *= 2
    return out


def kernel(
    ka_size, n, scale,
    slots_ref, count_ref, ec_ref, row_ref, ev_ref, tb_hbm, t2_hbm, cond_hbm,
    out_ref,
    tb, t2, cond, csend, cblk, vmsg, vals, hmsg, hrecv, allv, evm, mult, wrow, first, moved, wt,
    own, p0s, p0r, s1a, s1b, g1a, g1b, s2a, s2b, g2a, g2b, s3, g3,
    t_sem, k_sem, v_own, v_send, v_recv, l_send, l_recv, h_send, h_recv, c_send, c_recv,
    q0, r0, q1, r1, q2, r2, q3, r3,
):
    my_ka = lax.axis_index("ka")
    me = lax.axis_index("pair")
    core = lax.rem(my_ka, 2)
    kb = my_ka - core
    mz = me // 4
    zbit = lax.rem(mz, 2)
    sibling = kb + 1 - core
    slots = slots_ref.shape[0]
    bc = ec_ref.shape[1]
    hb = bc // 2
    pairs = slots // 2
    count = slots * bc
    hcount = count // 2
    rows = cond.shape[0]
    hr = rows // 2
    win = out_ref.shape[1]
    half = win // 2
    qw = half // 2
    groups = n // 4
    per_a = n // GA
    rb = GB // KG
    nval = ka_size * n
    home_owner = me + 4 * (core - zbit)
    at_home = core == zbit

    def remote(src, dst, ssem, rsem, ka, pair):
        return pltpu.make_async_remote_copy(
            src_ref=src, dst_ref=dst, send_sem=ssem, recv_sem=rsem,
            device_id=(ka, pair), device_id_type=MESH,
        )

    barrier = pltpu.get_barrier_semaphore()

    def greet(i, carry):
        other = lax.rem(me + i, n)
        for k in (my_ka, sibling):
            pl.semaphore_signal(barrier, inc=1, device_id=(k, other), device_id_type=MESH)
        return carry

    def greet_core(i, carry):
        pl.semaphore_signal(
            barrier, inc=1, device_id=(lax.rem(kb + i, ka_size), me), device_id_type=MESH
        )
        return carry

    cond_in = pltpu.make_async_copy(cond_hbm, cond, k_sem)
    cond_in.start()
    lax.fori_loop(1, n, greet, 0)
    pl.semaphore_signal(barrier, inc=1, device_id=(sibling, me), device_id_type=MESH)
    lax.fori_loop(2, ka_size, greet_core, 0)
    tables = (pltpu.make_async_copy(tb_hbm, tb, t_sem.at[0]), pltpu.make_async_copy(t2_hbm, t2, t_sem.at[1]))
    for copy in tables:
        copy.start()

    row = row_ref[...].astype(F32)
    grid_rows = [row[:, a * GB : (a + 1) * GB] for a in range(GA)]
    energy = jnp.broadcast_to(ev_ref[...].astype(F32), (8, GB))
    vmsg[...] = jnp.concatenate(grid_rows + [energy], axis=0).astype(BF16)
    own_val = pltpu.make_async_copy(vmsg, vals.at[my_ka, me], v_own)
    own_val.start()

    low = lax.broadcasted_iota(jnp.int32, (8, bc), 1) < hb
    low1 = lax.broadcasted_iota(jnp.int32, (1, bc), 1) < hb
    for t in range(pairs):
        hmsg[t : t + 1] = jnp.where(low1, slots_ref[2 * t], slots_ref[2 * t + 1]).astype(F32)
    ec = jnp.broadcast_to(ec_ref[...], (8, bc))
    turned = pltpu.roll(ec, hb, 1)
    hmsg[pairs : pairs + 8] = jnp.where(low, ec, turned)
    hmsg[pairs + 8 : pairs + 16] = jnp.where(low, turned, ec)
    hmsg[pairs + 16 : pairs + 24] = jnp.broadcast_to(count_ref[0], (8, bc)).astype(F32)

    cond_in.wait()
    low_c = lax.broadcasted_iota(jnp.int32, (hr, bc), 1) < hb

    def pack(o, carry):
        block = cond[:, pl.ds(pl.multiple_of(o * bc, bc), bc)].astype(F32)
        top, bot = block[:hr], block[hr:]
        csend[0, o] = jnp.where(low_c, top, pltpu.roll(bot, hb, 1)).astype(BF16)
        csend[1, o] = jnp.where(low_c, pltpu.roll(top, hb, 1), bot).astype(BF16)
        return carry

    lax.fori_loop(0, n, pack, 0, unroll=4)
    own_val.wait()

    pl.semaphore_wait(barrier, 2 * n - 1 + ka_size - 2)

    def send_val(i, carry):
        remote(vmsg, vals.at[my_ka, me], v_send, v_recv, my_ka, xor(me, i, n)).start()
        return carry

    lax.fori_loop(1, n, send_val, 0)

    home_copy = remote(hmsg, hrecv, h_send, h_recv, sibling, home_owner)

    @pl.when(at_home)
    def _():
        hrecv[...] = hmsg[...]

    @pl.when(jnp.logical_not(at_home))
    def _():
        home_copy.start()

    def cond_copy(h, o):
        obit = lax.rem(o // 4, 2)
        return remote(
            csend.at[h, o], cblk.at[h, me], c_send.at[h, o], c_recv.at[h, me],
            kb + obit, o + 4 * (core - obit),
        )

    def own_cond(h):
        return pltpu.make_async_copy(csend.at[h, me], cblk.at[h, me], c_recv.at[h, me])

    for h in range(2):
        @pl.when(at_home)
        def _():
            own_cond(h).start()

        @pl.when(jnp.logical_not(at_home))
        def _():
            cond_copy(h, me).start()

        def send_cond(i, carry):
            cond_copy(h, xor(me, i, n)).start()
            return carry

        lax.fori_loop(1, n, send_cond, 0)

    rest = vals.at[my_ka, pl.ds(0, n - 1)]
    pltpu.make_async_copy(rest, rest, v_recv).wait()

    def lane_copy(i):
        other = lax.rem(my_ka + i, ka_size)
        return remote(vals.at[my_ka], vals.at[my_ka], l_send.at[other], l_recv.at[my_ka], other, me)

    def send_lane(i, carry):
        lane_copy(i).start()
        return carry

    def wait_lane(i, carry):
        other = lax.rem(my_ka + i, ka_size)
        pltpu.make_async_copy(vals.at[other], vals.at[other], l_recv.at[other]).wait()
        return carry

    lax.fori_loop(1, ka_size, send_lane, 0)
    lax.fori_loop(1, ka_size, wait_lane, 0)

    @pl.when(jnp.logical_not(at_home))
    def _():
        home_copy.wait_recv()

    def unfold(v, carry):
        tile = vals[v // n, lax.rem(v, n)].astype(F32)
        allv[:, pl.ds(v, 1), :] = tile[:GA][:, None, :]
        evm[pl.ds(v, 1), :] = tile[GA : GA + 1]
        return carry

    lax.fori_loop(0, nval, unfold, 0, unroll=8)
    index = lax.broadcasted_iota(jnp.int32, (nval, bc), 0).astype(F32)
    hot = []
    for t in range(pairs):
        one = jnp.where(index == hrecv[t : t + 1], 1.0, 0.0)
        hot.append(one.astype(BF16))
        e_v = jnp.sum(one * evm[...], axis=0, keepdims=True)
        slot = jnp.where(low1, 2.0 * t, 2.0 * t + 1.0)
        live = jnp.where(slot < hrecv[pairs + 16 : pairs + 17], 1.0, 0.0)
        for h in range(2):
            e_c = hrecv[pairs + 8 * h : pairs + 8 * h + 1]
            wrow[0:1, h * hcount + t * bc : h * hcount + (t + 1) * bc] = live * 2.0 / (e_c - e_v)
    hot = jnp.concatenate(hot, axis=1)

    def spread(a, carry):
        mult[pl.ds(pl.multiple_of(a * GB, GB), GB), :] = lax.dot_general(
            allv[a].astype(BF16), hot, (((0,), (0,)), ((), ())), preferred_element_type=F32
        ).astype(BF16)
        return carry

    lax.fori_loop(0, GA, spread, 0, unroll=2)

    for copy in tables:
        copy.wait()
    home_a = home_owner // per_a
    wide = min(2 * bc, hcount)

    for h in range(2):
        def do_first(step, carry):
            for r in range(UNROLL_A):
                a = xor(home_a, step * UNROLL_A + r, GA)
                for q in range(per_a):
                    src = a * per_a + q
                    pltpu.make_async_copy(cblk.at[h, src], cblk.at[h, src], c_recv.at[h, src]).wait()
                tops, bots = [], []
                for q in range(per_a):
                    part = cblk[h, a * per_a + q].astype(F32)
                    turn = pltpu.roll(part, hb, 1)
                    tops.append(jnp.where(low_c, part, turn))
                    tops.append(jnp.where(low_c, turn, part))
                block = jnp.concatenate(tops, axis=0).astype(BF16)
                block = jnp.concatenate([block] * (wide // bc), axis=1)
                for at in range(0, hcount, wide):
                    x = block * mult[pl.ds(pl.multiple_of(a * GB, GB), GB), at : at + wide]
                    f = jnp.dot(tb[...], x, preferred_element_type=F32).astype(BF16)
                    for kg in range(KG):
                        first[kg, pl.ds(pl.multiple_of(a * rb, rb), rb), at : at + wide] = f[
                            kg * rb : (kg + 1) * rb
                        ]
            return carry

        lax.fori_loop(0, GA // UNROLL_A, do_first, 0)

        def do_moved(kg, carry):
            start = pl.multiple_of(kg * rb, rb)
            for at in range(0, hcount, wide):
                sl = slice(h * hcount + at, h * hcount + at + wide)
                mv = jnp.dot(t2[...], first[kg, :, at : at + wide], preferred_element_type=F32).astype(BF16)
                for j in range(GA):
                    piece = mv[j * rb : (j + 1) * rb]
                    moved[pl.ds(j * GB + start, rb), sl] = piece
                    if j * GB < win:
                        wt[pl.ds(j * GB + start, rb), sl] = (piece.astype(F32) * wrow[0:1, sl]).astype(BF16)
            return carry

        lax.fori_loop(0, KG, do_moved, 0, unroll=KG // 2)

    mx, my = lax.rem(me, 2), lax.rem(me, 4) // 2
    px, py = 1 - mx, 1 - my
    x_peer = mz * 4 + my * 2 + px
    y_peer = mz * 4 + py * 2 + mx

    def target(i):
        return lax.rem(mz + 1 + i, groups)

    def step0(i):
        return remote(p0s.at[i], p0r.at[i], q0.at[i], r0.at[i], sibling, me)

    def step1(i):
        return [
            remote(s1a.at[i, 0], g1a.at[i, 0], q1.at[0, i], r1.at[0, i], my_ka, x_peer),
            remote(s1b.at[i, 0], g1b.at[i, 0], q1.at[1, i], r1.at[1, i], my_ka, y_peer),
            remote(s1a.at[i, 1], g1a.at[i, 1], q1.at[2, i], r1.at[2, i], my_ka, x_peer),
            remote(s1b.at[i, 1], g1b.at[i, 1], q1.at[3, i], r1.at[3, i], my_ka, y_peer),
        ]

    def step2(i):
        return [
            remote(s2a.at[i], g2a.at[i], q2.at[0, i], r2.at[0, i], my_ka, y_peer),
            remote(s2b.at[i], g2b.at[i], q2.at[1, i], r2.at[1, i], my_ka, x_peer),
        ]

    def step3(i):
        return remote(
            s3.at[i], g3.at[mz // 2, core], q3.at[i], r3.at[mz // 2, core],
            kb + zbit, target(i) * 4 + lax.rem(me, 4),
        )

    def product(i, side):
        z = target(i)
        return lax.dot_general(
            moved[pl.ds(pl.multiple_of(z * 4 * rows, 4 * rows), 4 * rows), :],
            wt[pl.ds(pl.multiple_of(side * half, half), half), :],
            (((1,), (1,)), ((), ())), preferred_element_type=F32,
        )

    def pair_sum(i, y, x, b):
        at = pl.ds(pl.multiple_of((2 * y + x) * rows, rows), rows)
        sl = slice(b * qw, (b + 1) * qw)
        return own[i, at, sl] + p0r[i, at, sl].astype(F32)

    lag1, lag2, lag3 = LAGS

    def flow(i, carry):
        @pl.when(i < groups)
        def _():
            p0s[i] = product(i, 1 - core).astype(BF16)
            step0(i).start()

        @pl.when(i < groups)
        def _():
            own[i] = product(i, core)

        @pl.when((i >= lag1) & (i < groups + lag1))
        def _():
            t = i - lag1
            step0(t).wait_recv()
            copies = step1(t)
            s1a[t, 0] = pair_sum(t, py, px, 0).astype(BF16)
            copies[0].start()
            s1b[t, 0] = pair_sum(t, py, px, 1).astype(BF16)
            copies[1].start()
            s1a[t, 1] = pair_sum(t, my, px, 0).astype(BF16)
            copies[2].start()
            s1b[t, 1] = pair_sum(t, py, mx, 1).astype(BF16)
            copies[3].start()

        @pl.when((i >= lag2) & (i < groups + lag2))
        def _():
            t = i - lag2
            first_copies, copies = step1(t), step2(t)
            first_copies[0].wait_recv()
            s2a[t] = (pair_sum(t, py, mx, 0) + g1a[t, 0].astype(F32)).astype(BF16)
            copies[0].start()
            first_copies[1].wait_recv()
            s2b[t] = (pair_sum(t, my, px, 1) + g1b[t, 0].astype(F32)).astype(BF16)
            copies[1].start()

        @pl.when((i >= lag3) & (i < groups + lag3))
        def _():
            t = i - lag3
            first_copies, second_copies = step1(t), step2(t)
            first_copies[2].wait_recv()
            first_copies[3].wait_recv()
            second_copies[0].wait_recv()
            a = pair_sum(t, my, mx, 0) + g1a[t, 1].astype(F32) + g2a[t].astype(F32)
            second_copies[1].wait_recv()
            b = pair_sum(t, my, mx, 1) + g1b[t, 1].astype(F32) + g2b[t].astype(F32)
            a, b = a.astype(BF16), b.astype(BF16)
            stays = at_home & (t == groups - 1)

            @pl.when(stays)
            def _():
                g3[mz // 2, core, :, :qw] = a
                g3[mz // 2, core, :, qw:] = b

            @pl.when(jnp.logical_not(stays))
            def _():
                s3[t, :, :qw] = a
                s3[t, :, qw:] = b
                step3(t).start()

        return carry

    lax.fori_loop(0, groups + lag3, flow, 0)

    for q in range(2):
        for w in range(groups // 2):
            mine = at_home & (w == mz // 2) & (q == core)

            @pl.when(jnp.logical_not(mine))
            def _():
                pltpu.make_async_copy(g3.at[w, q], g3.at[w, q], r3.at[w, q]).wait()

        total = g3[0, q].astype(F32)
        for w in range(1, groups // 2):
            total = total + g3[w, q].astype(F32)
        out_ref[:, q * half : (q + 1) * half] = total * scale

    pltpu.make_async_copy(rest, rest, v_send).wait()

    @pl.when(jnp.logical_not(at_home))
    def _():
        home_copy.wait_send()

    for h in range(2):
        @pl.when(jnp.logical_not(at_home))
        def _():
            cond_copy(h, me).wait_send()

        def drain_cond(i, carry):
            cond_copy(h, xor(me, i, n)).wait_send()
            return carry

        lax.fori_loop(1, n, drain_cond, 0)

    def drain_lane(i, carry):
        lane_copy(i).wait_send()
        return carry

    lax.fori_loop(1, ka_size, drain_lane, 0)

    def drain(i, carry):
        for copy in [step0(i)] + step1(i) + step2(i):
            copy.wait_send()

        @pl.when(jnp.logical_not(at_home & (i == groups - 1)))
        def _():
            step3(i).wait_send()

        return carry

    lax.fori_loop(0, groups, drain, 0)


def shards(ka_size, n, cond_orbitals, cond_energy, val_orbitals, val_energy, val_slots, owner_count):
    cond = cond_orbitals[0]
    rows, bc = cond.shape[0], cond.shape[1] // n
    slots = val_slots.shape[2]
    win = 4 * GB
    half = win // 2
    grid = GA * GB
    count = slots * bc
    hcount = count // 2
    groups = n // 4
    nval = ka_size * n
    rb = GB // KG
    table_b = cosine_table(GB)
    table_2 = np.kron(cosine_table(GA), np.eye(rb, dtype=np.float32)).astype(jnp.bfloat16)
    scale = 2.0 / (slots * bc * n)
    vmem = pl.BlockSpec(memory_space=pltpu.VMEM)
    smem = pl.BlockSpec(memory_space=pltpu.SMEM)
    hbm = pl.BlockSpec(memory_space=pl.ANY)
    dma = pltpu.SemaphoreType.DMA
    out = pl.pallas_call(
        functools.partial(kernel, ka_size, n, scale),
        out_shape=jax.ShapeDtypeStruct((rows, win), F32),
        in_specs=[smem, smem, vmem, vmem, vmem, hbm, hbm, hbm],
        out_specs=vmem,
        scratch_shapes=[
            pltpu.VMEM((GB, GB), BF16),
            pltpu.VMEM((GA * rb, GA * rb), BF16),
            pltpu.VMEM((rows, n * bc), BF16),
            pltpu.VMEM((2, n, rows // 2, bc), BF16),
            pltpu.VMEM((2, n, rows // 2, bc), BF16),
            pltpu.VMEM((GA + 8, GB), BF16),
            pltpu.VMEM((ka_size, n, GA + 8, GB), BF16),
            pltpu.VMEM((slots // 2 + 24, bc), F32),
            pltpu.VMEM((slots // 2 + 24, bc), F32),
            pltpu.VMEM((GA, nval, GB), F32),
            pltpu.VMEM((nval, GB), F32),
            pltpu.VMEM((grid, hcount), BF16),
            pltpu.VMEM((8, count), F32),
            pltpu.VMEM((KG, GA * rb, hcount), BF16),
            pltpu.VMEM((grid, count), BF16),
            pltpu.VMEM((win, count), BF16),
            pltpu.VMEM((groups, 4 * rows, half), F32),
            pltpu.VMEM((groups, 4 * rows, half), BF16),
            pltpu.VMEM((groups, 4 * rows, half), BF16),
            *[pltpu.VMEM((groups, 2, rows, half // 2), BF16)] * 4,
            *[pltpu.VMEM((groups, rows, half // 2), BF16)] * 4,
            pltpu.VMEM((groups, rows, half), BF16),
            pltpu.VMEM((groups // 2, 2, rows, half), BF16),
            dma((2,)), dma(()), dma(()), dma(()), dma(()), dma((ka_size,)), dma((ka_size,)), dma(()), dma(()),
            dma((2, n)), dma((2, n)),
            dma((groups,)), dma((groups,)), dma((4, groups)), dma((4, groups)), dma((2, groups)), dma((2, groups)),
            dma((groups,)), dma((groups // 2, 2)),
        ],
        compiler_params=pltpu.CompilerParams(
            collective_id=0, has_side_effects=True, vmem_limit_bytes=60 * 1024 * 1024
        ),
        name="polarizability",
    )(
        val_slots[0, 0], owner_count[0], cond_energy, val_orbitals, val_energy[:, None],
        jnp.asarray(table_b), jnp.asarray(table_2), cond,
    )
    return out[None]


def solution(mesh):
    return jax.shard_map(
        functools.partial(shards, mesh.shape["ka"], mesh.shape["pair"]),
        mesh=mesh,
        in_specs=(
            P("ka", "pair", None),
            P("ka", "pair"),
            P(("ka", "pair"), None),
            P(("ka", "pair")),
            P("ka", "pair", None),
            P("ka", "pair"),
        ),
        out_specs=P("ka", "pair", None),
        check_vma=False,
    )
```

```python
import functools

import jax
import jax.numpy as jnp
import numpy as np
from jax import lax
from jax.experimental import pallas as pl
from jax.experimental.pallas import tpu as pltpu
from jax.sharding import PartitionSpec as P

GA = 16
GB = 128
KG = 8
UNROLL_A = 4
MESH = pl.DeviceIdType.MESH
F32 = jnp.float32
BF16 = jnp.bfloat16


def cosine_table(length):
    freq = np.arange(length, dtype=np.float32)[:, None]
    point = np.arange(length, dtype=np.float32)[None, :]
    factor = np.where(freq == 0, np.sqrt(np.float32(1.0 / length)), np.sqrt(np.float32(2.0 / length)))
    angle = np.float32(np.pi) * (point + np.float32(0.5)) * freq / np.float32(length)
    return (factor * np.cos(angle)).astype(jnp.bfloat16)


def xor(value, other, limit):
    out, bit = 0, 1
    while bit < limit:
        out = out + lax.rem(value // bit + other // bit, 2) * bit
        bit *= 2
    return out


def kernel(
    ka_size, n, scale,
    slots_ref, count_ref, ec_ref, row_ref, ev_ref, tb_hbm, t2_hbm, cond_hbm,
    out_ref,
    tb, t2, cond, csend, cblk, vmsg, vals, hmsg, hrecv, allv, evm, mult, wrow, first, moved, wt,
    own, p0s, p0r, s1a, s1b, g1a, g1b, s2a, s2b, g2a, g2b, s3, g3,
    t_sem, k_sem, v_own, v_send, v_recv, l_send, l_recv, h_send, h_recv, c_send, c_recv,
    q0, r0, q1, r1, q2, r2, q3, r3,
):
    my_ka = lax.axis_index("ka")
    me = lax.axis_index("pair")
    core = lax.rem(my_ka, 2)
    kb = my_ka - core
    mz = me // 4
    zbit = lax.rem(mz, 2)
    sibling = kb + 1 - core
    slots = slots_ref.shape[0]
    bc = ec_ref.shape[1]
    hb = bc // 2
    pairs = slots // 2
    count = slots * bc
    hcount = count // 2
    rows = cond.shape[0]
    hr = rows // 2
    win = out_ref.shape[1]
    half = win // 2
    qw = half // 2
    groups = n // 4
    per_a = n // GA
    rb = GB // KG
    nval = ka_size * n
    home_owner = me + 4 * (core - zbit)
    at_home = core == zbit

    def remote(src, dst, ssem, rsem, ka, pair):
        return pltpu.make_async_remote_copy(
            src_ref=src, dst_ref=dst, send_sem=ssem, recv_sem=rsem,
            device_id=(ka, pair), device_id_type=MESH,
        )

    barrier = pltpu.get_barrier_semaphore()

    def greet(i, carry):
        other = lax.rem(me + i, n)
        for k in (my_ka, sibling):
            pl.semaphore_signal(barrier, inc=1, device_id=(k, other), device_id_type=MESH)
        return carry

    def greet_core(i, carry):
        pl.semaphore_signal(
            barrier, inc=1, device_id=(lax.rem(kb + i, ka_size), me), device_id_type=MESH
        )
        return carry

    cond_in = pltpu.make_async_copy(cond_hbm, cond, k_sem)
    cond_in.start()
    lax.fori_loop(1, n, greet, 0)
    pl.semaphore_signal(barrier, inc=1, device_id=(sibling, me), device_id_type=MESH)
    lax.fori_loop(2, ka_size, greet_core, 0)
    tables = (pltpu.make_async_copy(tb_hbm, tb, t_sem.at[0]), pltpu.make_async_copy(t2_hbm, t2, t_sem.at[1]))
    for copy in tables:
        copy.start()

    row = row_ref[...].astype(F32)
    grid_rows = [row[:, a * GB : (a + 1) * GB] for a in range(GA)]
    energy = jnp.broadcast_to(ev_ref[...].astype(F32), (8, GB))
    vmsg[...] = jnp.concatenate(grid_rows + [energy], axis=0).astype(BF16)
    own_val = pltpu.make_async_copy(vmsg, vals.at[my_ka, me], v_own)
    own_val.start()

    low = lax.broadcasted_iota(jnp.int32, (8, bc), 1) < hb
    low1 = lax.broadcasted_iota(jnp.int32, (1, bc), 1) < hb
    for t in range(pairs):
        hmsg[t : t + 1] = jnp.where(low1, slots_ref[2 * t], slots_ref[2 * t + 1]).astype(F32)
    ec = jnp.broadcast_to(ec_ref[...], (8, bc))
    turned = pltpu.roll(ec, hb, 1)
    hmsg[pairs : pairs + 8] = jnp.where(low, ec, turned)
    hmsg[pairs + 8 : pairs + 16] = jnp.where(low, turned, ec)
    hmsg[pairs + 16 : pairs + 24] = jnp.broadcast_to(count_ref[0], (8, bc)).astype(F32)

    cond_in.wait()
    low_c = lax.broadcasted_iota(jnp.int32, (hr, bc), 1) < hb

    def pack(o, carry):
        block = cond[:, pl.ds(pl.multiple_of(o * bc, bc), bc)].astype(F32)
        top, bot = block[:hr], block[hr:]
        csend[0, o] = jnp.where(low_c, top, pltpu.roll(bot, hb, 1)).astype(BF16)
        csend[1, o] = jnp.where(low_c, pltpu.roll(top, hb, 1), bot).astype(BF16)
        return carry

    lax.fori_loop(0, n, pack, 0, unroll=4)
    own_val.wait()

    pl.semaphore_wait(barrier, 2 * n - 1 + ka_size - 2)

    def send_val(i, carry):
        remote(vmsg, vals.at[my_ka, me], v_send, v_recv, my_ka, xor(me, i, n)).start()
        return carry

    lax.fori_loop(1, n, send_val, 0)

    home_copy = remote(hmsg, hrecv, h_send, h_recv, sibling, home_owner)

    @pl.when(at_home)
    def _():
        hrecv[...] = hmsg[...]

    @pl.when(jnp.logical_not(at_home))
    def _():
        home_copy.start()

    def cond_copy(h, o):
        obit = lax.rem(o // 4, 2)
        return remote(
            csend.at[h, o], cblk.at[h, me], c_send.at[h, o], c_recv.at[h, me],
            kb + obit, o + 4 * (core - obit),
        )

    def own_cond(h):
        return pltpu.make_async_copy(csend.at[h, me], cblk.at[h, me], c_recv.at[h, me])

    def send_half(h):
        @pl.when(at_home)
        def _():
            own_cond(h).start()

        @pl.when(jnp.logical_not(at_home))
        def _():
            cond_copy(h, me).start()

        def send_cond(i, carry):
            cond_copy(h, xor(me, i, n)).start()
            return carry

        lax.fori_loop(1, n, send_cond, 0)

    send_half(0)
    rest = vals.at[my_ka, pl.ds(0, n - 1)]
    pltpu.make_async_copy(rest, rest, v_recv).wait()

    def lane_copy(i):
        other = lax.rem(my_ka + i, ka_size)
        return remote(vals.at[my_ka], vals.at[my_ka], l_send.at[other], l_recv.at[my_ka], other, me)

    def send_lane(i, carry):
        lane_copy(i).start()
        return carry

    def wait_lane(i, carry):
        other = lax.rem(my_ka + i, ka_size)
        pltpu.make_async_copy(vals.at[other], vals.at[other], l_recv.at[other]).wait()
        return carry

    lax.fori_loop(1, ka_size, send_lane, 0)
    lax.fori_loop(1, ka_size, wait_lane, 0)

    @pl.when(jnp.logical_not(at_home))
    def _():
        home_copy.wait_recv()

    send_half(1)

    def unfold(v, carry):
        tile = vals[v // n, lax.rem(v, n)].astype(F32)
        allv[:, pl.ds(v, 1), :] = tile[:GA][:, None, :]
        evm[pl.ds(v, 1), :] = tile[GA : GA + 1]
        return carry

    lax.fori_loop(0, nval, unfold, 0, unroll=8)
    index = lax.broadcasted_iota(jnp.int32, (nval, bc), 0).astype(F32)
    hot = []
    for t in range(pairs):
        one = jnp.where(index == hrecv[t : t + 1], 1.0, 0.0)
        hot.append(one.astype(BF16))
        e_v = jnp.sum(one * evm[...], axis=0, keepdims=True)
        slot = jnp.where(low1, 2.0 * t, 2.0 * t + 1.0)
        live = jnp.where(slot < hrecv[pairs + 16 : pairs + 17], 1.0, 0.0)
        for h in range(2):
            e_c = hrecv[pairs + 8 * h : pairs + 8 * h + 1]
            wrow[0:1, h * hcount + t * bc : h * hcount + (t + 1) * bc] = live * 2.0 / (e_c - e_v)
    hot = jnp.concatenate(hot, axis=1)

    def spread(a, carry):
        mult[pl.ds(pl.multiple_of(a * GB, GB), GB), :] = lax.dot_general(
            allv[a].astype(BF16), hot, (((0,), (0,)), ((), ())), preferred_element_type=F32
        ).astype(BF16)
        return carry

    lax.fori_loop(0, GA, spread, 0, unroll=2)

    for copy in tables:
        copy.wait()
    home_a = home_owner // per_a
    wide = min(2 * bc, hcount)

    for h in range(2):
        def do_first(step, carry):
            for r in range(UNROLL_A):
                a = xor(home_a, step * UNROLL_A + r, GA)
                for q in range(per_a):
                    src = a * per_a + q
                    pltpu.make_async_copy(cblk.at[h, src], cblk.at[h, src], c_recv.at[h, src]).wait()
                tops, bots = [], []
                for q in range(per_a):
                    part = cblk[h, a * per_a + q].astype(F32)
                    turn = pltpu.roll(part, hb, 1)
                    tops.append(jnp.where(low_c, part, turn))
                    tops.append(jnp.where(low_c, turn, part))
                block = jnp.concatenate(tops, axis=0).astype(BF16)
                block = jnp.concatenate([block] * (wide // bc), axis=1)
                for at in range(0, hcount, wide):
                    x = block * mult[pl.ds(pl.multiple_of(a * GB, GB), GB), at : at + wide]
                    f = jnp.dot(tb[...], x, preferred_element_type=F32).astype(BF16)
                    for kg in range(KG):
                        first[kg, pl.ds(pl.multiple_of(a * rb, rb), rb), at : at + wide] = f[
                            kg * rb : (kg + 1) * rb
                        ]
            return carry

        lax.fori_loop(0, GA // UNROLL_A, do_first, 0)

        def do_moved(kg, carry):
            start = pl.multiple_of(kg * rb, rb)
            for at in range(0, hcount, wide):
                sl = slice(h * hcount + at, h * hcount + at + wide)
                mv = jnp.dot(t2[...], first[kg, :, at : at + wide], preferred_element_type=F32).astype(BF16)
                for j in range(GA):
                    piece = mv[j * rb : (j + 1) * rb]
                    moved[pl.ds(j * GB + start, rb), sl] = piece
                    if j * GB < win:
                        wt[pl.ds(j * GB + start, rb), sl] = (piece.astype(F32) * wrow[0:1, sl]).astype(BF16)
            return carry

        lax.fori_loop(0, KG, do_moved, 0, unroll=KG // 2)

    mx, my = lax.rem(me, 2), lax.rem(me, 4) // 2
    px, py = 1 - mx, 1 - my
    x_peer = mz * 4 + my * 2 + px
    y_peer = mz * 4 + py * 2 + mx

    def target(i):
        return lax.rem(mz + 1 + i, groups)

    def step0(i):
        return remote(p0s.at[i], p0r.at[i], q0.at[i], r0.at[i], sibling, me)

    def step1(i):
        return [
            remote(s1a.at[i, 0], g1a.at[i, 0], q1.at[0, i], r1.at[0, i], my_ka, x_peer),
            remote(s1b.at[i, 0], g1b.at[i, 0], q1.at[1, i], r1.at[1, i], my_ka, y_peer),
            remote(s1a.at[i, 1], g1a.at[i, 1], q1.at[2, i], r1.at[2, i], my_ka, x_peer),
            remote(s1b.at[i, 1], g1b.at[i, 1], q1.at[3, i], r1.at[3, i], my_ka, y_peer),
        ]

    def step2(i):
        return [
            remote(s2a.at[i], g2a.at[i], q2.at[0, i], r2.at[0, i], my_ka, y_peer),
            remote(s2b.at[i], g2b.at[i], q2.at[1, i], r2.at[1, i], my_ka, x_peer),
        ]

    def step3(i):
        return remote(
            s3.at[i], g3.at[mz // 2, core], q3.at[i], r3.at[mz // 2, core],
            kb + zbit, target(i) * 4 + lax.rem(me, 4),
        )

    def product(i, side):
        z = target(i)
        return lax.dot_general(
            moved[pl.ds(pl.multiple_of(z * 4 * rows, 4 * rows), 4 * rows), :],
            wt[pl.ds(pl.multiple_of(side * half, half), half), :],
            (((1,), (1,)), ((), ())), preferred_element_type=F32,
        )

    def pair_sum(i, y, x, b):
        at = pl.ds(pl.multiple_of((2 * y + x) * rows, rows), rows)
        sl = slice(b * qw, (b + 1) * qw)
        return own[i, at, sl] + p0r[i, at, sl].astype(F32)

    def other_half(i):
        p0s[i] = product(i, 1 - core).astype(BF16)
        step0(i).start()

    def own_half(i):
        own[i] = product(i, core)

    def after0(i):
        step0(i).wait_recv()
        copies = step1(i)
        s1a[i, 0] = pair_sum(i, py, px, 0).astype(BF16)
        copies[0].start()
        s1b[i, 0] = pair_sum(i, py, px, 1).astype(BF16)
        copies[1].start()
        s1a[i, 1] = pair_sum(i, my, px, 0).astype(BF16)
        copies[2].start()
        s1b[i, 1] = pair_sum(i, py, mx, 1).astype(BF16)
        copies[3].start()

    def after1(i):
        first_copies, copies = step1(i), step2(i)
        first_copies[0].wait_recv()
        s2a[i] = (pair_sum(i, py, mx, 0) + g1a[i, 0].astype(F32)).astype(BF16)
        copies[0].start()
        first_copies[1].wait_recv()
        s2b[i] = (pair_sum(i, my, px, 1) + g1b[i, 0].astype(F32)).astype(BF16)
        copies[1].start()

    def after2(i):
        first_copies, second_copies = step1(i), step2(i)
        first_copies[2].wait_recv()
        first_copies[3].wait_recv()
        second_copies[0].wait_recv()
        a = pair_sum(i, my, mx, 0) + g1a[i, 1].astype(F32) + g2a[i].astype(F32)
        second_copies[1].wait_recv()
        b = pair_sum(i, my, mx, 1) + g1b[i, 1].astype(F32) + g2b[i].astype(F32)
        a, b = a.astype(BF16), b.astype(BF16)
        stays = at_home & (i == groups - 1)

        @pl.when(stays)
        def _():
            g3[mz // 2, core, :, :qw] = a
            g3[mz // 2, core, :, qw:] = b

        @pl.when(jnp.logical_not(stays))
        def _():
            s3[i, :, :qw] = a
            s3[i, :, qw:] = b
            step3(i).start()

    if groups == 4:
        order = (
            (other_half, 0), (own_half, 0), (other_half, 1), (after0, 0), (own_half, 1), (other_half, 2),
            (after0, 1), (own_half, 2), (other_half, 3), (after0, 2), (after1, 0), (own_half, 3), (after0, 3),
            (after1, 1), (after1, 2), (after2, 0), (after1, 3), (after2, 1), (after2, 2), (after2, 3),
        )
        for stage, i in order:
            stage(i)
    else:
        def flow(i, carry):
            for stage, lag in ((other_half, 0), (own_half, 0), (after0, 1), (after1, 3), (after2, 4)):
                @pl.when((i >= lag) & (i < groups + lag))
                def _():
                    stage(i - lag)

            return carry

        lax.fori_loop(0, groups + 4, flow, 0)

    for q in range(2):
        for w in range(groups // 2):
            mine = at_home & (w == mz // 2) & (q == core)

            @pl.when(jnp.logical_not(mine))
            def _():
                pltpu.make_async_copy(g3.at[w, q], g3.at[w, q], r3.at[w, q]).wait()

        total = g3[0, q].astype(F32)
        for w in range(1, groups // 2):
            total = total + g3[w, q].astype(F32)
        out_ref[:, q * half : (q + 1) * half] = total * scale

    pltpu.make_async_copy(rest, rest, v_send).wait()

    @pl.when(jnp.logical_not(at_home))
    def _():
        home_copy.wait_send()

    for h in range(2):
        @pl.when(jnp.logical_not(at_home))
        def _():
            cond_copy(h, me).wait_send()

        def drain_cond(i, carry):
            cond_copy(h, xor(me, i, n)).wait_send()
            return carry

        lax.fori_loop(1, n, drain_cond, 0)

    def drain_lane(i, carry):
        lane_copy(i).wait_send()
        return carry

    lax.fori_loop(1, ka_size, drain_lane, 0)

    def drain(i, carry):
        for copy in [step0(i)] + step1(i) + step2(i):
            copy.wait_send()

        @pl.when(jnp.logical_not(at_home & (i == groups - 1)))
        def _():
            step3(i).wait_send()

        return carry

    lax.fori_loop(0, groups, drain, 0)


def shards(ka_size, n, cond_orbitals, cond_energy, val_orbitals, val_energy, val_slots, owner_count):
    cond = cond_orbitals[0]
    rows, bc = cond.shape[0], cond.shape[1] // n
    slots = val_slots.shape[2]
    win = 4 * GB
    half = win // 2
    grid = GA * GB
    count = slots * bc
    hcount = count // 2
    groups = n // 4
    nval = ka_size * n
    rb = GB // KG
    table_b = cosine_table(GB)
    table_2 = np.kron(cosine_table(GA), np.eye(rb, dtype=np.float32)).astype(jnp.bfloat16)
    scale = 2.0 / (slots * bc * n)
    vmem = pl.BlockSpec(memory_space=pltpu.VMEM)
    smem = pl.BlockSpec(memory_space=pltpu.SMEM)
    hbm = pl.BlockSpec(memory_space=pl.ANY)
    dma = pltpu.SemaphoreType.DMA
    out = pl.pallas_call(
        functools.partial(kernel, ka_size, n, scale),
        out_shape=pltpu.VMEM((rows, win), F32),
        in_specs=[smem, smem, vmem, vmem, vmem, hbm, hbm, hbm],
        out_specs=vmem,
        scratch_shapes=[
            pltpu.VMEM((GB, GB), BF16),
            pltpu.VMEM((GA * rb, GA * rb), BF16),
            pltpu.VMEM((rows, n * bc), BF16),
            pltpu.VMEM((2, n, rows // 2, bc), BF16),
            pltpu.VMEM((2, n, rows // 2, bc), BF16),
            pltpu.VMEM((GA + 8, GB), BF16),
            pltpu.VMEM((ka_size, n, GA + 8, GB), BF16),
            pltpu.VMEM((slots // 2 + 24, bc), F32),
            pltpu.VMEM((slots // 2 + 24, bc), F32),
            pltpu.VMEM((GA, nval, GB), F32),
            pltpu.VMEM((nval, GB), F32),
            pltpu.VMEM((grid, hcount), BF16),
            pltpu.VMEM((8, count), F32),
            pltpu.VMEM((KG, GA * rb, hcount), BF16),
            pltpu.VMEM((grid, count), BF16),
            pltpu.VMEM((win, count), BF16),
            pltpu.VMEM((groups, 4 * rows, half), F32),
            pltpu.VMEM((groups, 4 * rows, half), BF16),
            pltpu.VMEM((groups, 4 * rows, half), BF16),
            *[pltpu.VMEM((groups, 2, rows, half // 2), BF16)] * 4,
            *[pltpu.VMEM((groups, rows, half // 2), BF16)] * 4,
            pltpu.VMEM((groups, rows, half), BF16),
            pltpu.VMEM((groups // 2, 2, rows, half), BF16),
            dma((2,)), dma(()), dma(()), dma(()), dma(()), dma((ka_size,)), dma((ka_size,)), dma(()), dma(()),
            dma((2, n)), dma((2, n)),
            dma((groups,)), dma((groups,)), dma((4, groups)), dma((4, groups)), dma((2, groups)), dma((2, groups)),
            dma((groups,)), dma((groups // 2, 2)),
        ],
        compiler_params=pltpu.CompilerParams(
            collective_id=0, has_side_effects=True, vmem_limit_bytes=60 * 1024 * 1024
        ),
        name="polarizability",
    )(
        val_slots[0, 0], owner_count[0], cond_energy, val_orbitals, val_energy[:, None],
        jnp.asarray(table_b), jnp.asarray(table_2), cond,
    )
    return out[None]


def solution(mesh):
    return jax.shard_map(
        functools.partial(shards, mesh.shape["ka"], mesh.shape["pair"]),
        mesh=mesh,
        in_specs=(
            P("ka", "pair", None),
            P("ka", "pair"),
            P(("ka", "pair"), None),
            P(("ka", "pair")),
            P("ka", "pair", None),
            P("ka", "pair"),
        ),
        out_specs=P("ka", "pair", None),
        check_vma=False,
    )
```

```python
import functools

import jax
import jax.numpy as jnp
import numpy as np
from jax import lax
from jax.experimental import pallas as pl
from jax.experimental.pallas import tpu as pltpu
from jax.sharding import PartitionSpec as P

GA = 16
GB = 128
KG = 8
UNROLL_A = (8, 8)
MESH = pl.DeviceIdType.MESH
F32 = jnp.float32
BF16 = jnp.bfloat16


def cosine_table(length):
    freq = np.arange(length, dtype=np.float32)[:, None]
    point = np.arange(length, dtype=np.float32)[None, :]
    factor = np.where(freq == 0, np.sqrt(np.float32(1.0 / length)), np.sqrt(np.float32(2.0 / length)))
    angle = np.float32(np.pi) * (point + np.float32(0.5)) * freq / np.float32(length)
    return (factor * np.cos(angle)).astype(jnp.bfloat16)


def xor(value, other, limit):
    out, bit = 0, 1
    while bit < limit:
        out = out + lax.rem(value // bit + other // bit, 2) * bit
        bit *= 2
    return out


def kernel(
    ka_size, n, scale,
    slots_ref, count_ref, ec_ref, row_ref, ev_ref, tb_hbm, t2_hbm, cond_hbm,
    out_ref,
    tb, t2, cond, csend, cblk, vmsg, vals, hmsg, hrecv, allv, evm, mult, wrow, first, moved, wt,
    own, p0s, p0r, s1a, s1b, g1a, g1b, s2a, s2b, g2a, g2b, s3, g3, sd, gd,
    t_sem, k_sem, v_own, v_send, v_recv, p_send, p_recv, l_send, l_recv, h_send, h_recv, c_send, c_recv,
    q0, r0, q1, r1, q2, r2, q3, r3, qd, rd,
):
    my_ka = lax.axis_index("ka")
    me = lax.axis_index("pair")
    core = lax.rem(my_ka, 2)
    kb = my_ka - core
    mz = me // 4
    xy = lax.rem(me, 4)
    zbit = lax.rem(mz, 2)
    sibling = kb + 1 - core
    slots = slots_ref.shape[0]
    bc = ec_ref.shape[1]
    hb = bc // 2
    pairs = slots // 2
    count = slots * bc
    hcount = count // 2
    rows = cond.shape[0]
    hr = rows // 2
    win = out_ref.shape[1]
    half = win // 2
    qw = half // 2
    groups = n // 4
    per_a = n // GA
    rb = GB // KG
    nval = ka_size * n
    home_owner = me + 4 * (core - zbit)
    at_home = core == zbit

    def remote(src, dst, ssem, rsem, ka, pair):
        return pltpu.make_async_remote_copy(
            src_ref=src, dst_ref=dst, send_sem=ssem, recv_sem=rsem,
            device_id=(ka, pair), device_id_type=MESH,
        )

    barrier = pltpu.get_barrier_semaphore()

    def greet(i, carry):
        other = lax.rem(me + i, n)
        for k in (my_ka, sibling):
            pl.semaphore_signal(barrier, inc=1, device_id=(k, other), device_id_type=MESH)
        return carry

    def greet_core(i, carry):
        pl.semaphore_signal(
            barrier, inc=1, device_id=(lax.rem(kb + i, ka_size), me), device_id_type=MESH
        )
        return carry

    cond_in = pltpu.make_async_copy(cond_hbm, cond, k_sem)
    cond_in.start()
    lax.fori_loop(1, n, greet, 0)
    pl.semaphore_signal(barrier, inc=1, device_id=(sibling, me), device_id_type=MESH)
    lax.fori_loop(2, ka_size, greet_core, 0)
    tables = (pltpu.make_async_copy(tb_hbm, tb, t_sem.at[0]), pltpu.make_async_copy(t2_hbm, t2, t_sem.at[1]))
    for copy in tables:
        copy.start()

    row = row_ref[...].astype(F32)
    grid_rows = [row[:, a * GB : (a + 1) * GB] for a in range(GA)]
    energy = jnp.broadcast_to(ev_ref[...].astype(F32), (8, GB))
    vmsg[...] = jnp.concatenate(grid_rows + [energy], axis=0).astype(BF16)
    own_val = pltpu.make_async_copy(vmsg, vals.at[my_ka, mz, xy], v_own)
    own_val.start()

    low = lax.broadcasted_iota(jnp.int32, (8, bc), 1) < hb
    low1 = lax.broadcasted_iota(jnp.int32, (1, bc), 1) < hb
    for t in range(pairs):
        hmsg[t : t + 1] = jnp.where(low1, slots_ref[2 * t], slots_ref[2 * t + 1]).astype(F32)
    ec = jnp.broadcast_to(ec_ref[...], (8, bc))
    turned = pltpu.roll(ec, hb, 1)
    hmsg[pairs : pairs + 8] = jnp.where(low, ec, turned)
    hmsg[pairs + 8 : pairs + 16] = jnp.where(low, turned, ec)
    hmsg[pairs + 16 : pairs + 24] = jnp.broadcast_to(count_ref[0], (8, bc)).astype(F32)

    cond_in.wait()
    low_c = lax.broadcasted_iota(jnp.int32, (hr, bc), 1) < hb

    def pack(o, carry):
        block = cond[:, pl.ds(pl.multiple_of(o * bc, bc), bc)].astype(F32)
        top, bot = block[:hr], block[hr:]
        csend[0, o] = jnp.where(low_c, top, pltpu.roll(bot, hb, 1)).astype(BF16)
        csend[1, o] = jnp.where(low_c, pltpu.roll(top, hb, 1), bot).astype(BF16)
        return carry

    lax.fori_loop(0, n, pack, 0, unroll=4)
    own_val.wait()

    pl.semaphore_wait(barrier, 2 * n - 1 + ka_size - 2)

    def send_val(i, carry):
        remote(
            vmsg, vals.at[my_ka, mz, xy], v_send, v_recv, my_ka, lax.rem(mz + i, groups) * 4 + xy
        ).start()
        return carry

    lax.fori_loop(1, groups, send_val, 0)
    column = vals.at[my_ka, pl.ds(0, groups), xy]
    rest = vals.at[my_ka, pl.ds(0, groups - 1), xy]

    def plane_copy(i):
        return remote(column, column, p_send.at[i], p_recv.at[i], my_ka, mz * 4 + xor(xy, i, 4))

    home_copy = remote(hmsg, hrecv, h_send, h_recv, sibling, home_owner)

    @pl.when(at_home)
    def _():
        hrecv[...] = hmsg[...]

    @pl.when(jnp.logical_not(at_home))
    def _():
        home_copy.start()

    def cond_copy(h, o):
        obit = lax.rem(o // 4, 2)
        return remote(
            csend.at[h, o], cblk.at[h, me], c_send.at[h, o], c_recv.at[h, me],
            kb + obit, o + 4 * (core - obit),
        )

    def own_cond(h):
        return pltpu.make_async_copy(csend.at[h, me], cblk.at[h, me], c_recv.at[h, me])

    def send_low(h):
        @pl.when(at_home)
        def _():
            own_cond(h).start()

        @pl.when(jnp.logical_not(at_home))
        def _():
            cond_copy(h, me).start()

        lax.fori_loop(1, n // 2, functools.partial(send_cond, h), 0)

    def send_cond(h, i, carry):
        cond_copy(h, lax.rem(me + i, n)).start()
        return carry

    def send_high(h):
        lax.fori_loop(n // 2, n, functools.partial(send_cond, h), 0)

    send_low(0)
    send_high(0)
    pltpu.make_async_copy(rest, rest, v_recv).wait()
    for i in range(1, 4):
        plane_copy(i).start()
    send_low(1)
    send_high(1)
    for i in range(1, 4):
        peer = vals.at[my_ka, pl.ds(0, groups), xor(xy, i, 4)]
        pltpu.make_async_copy(peer, peer, p_recv.at[i]).wait()

    def lane_copy(i):
        other = lax.rem(my_ka + i, ka_size)
        return remote(vals.at[my_ka], vals.at[my_ka], l_send.at[other], l_recv.at[my_ka], other, me)

    def send_lane(i, carry):
        lane_copy(i).start()
        return carry

    def wait_lane(i, carry):
        other = lax.rem(my_ka + i, ka_size)
        pltpu.make_async_copy(vals.at[other], vals.at[other], l_recv.at[other]).wait()
        return carry

    lax.fori_loop(1, ka_size, send_lane, 0)
    lax.fori_loop(1, ka_size, wait_lane, 0)

    @pl.when(jnp.logical_not(at_home))
    def _():
        home_copy.wait_recv()

    def unfold(v, carry):
        tile = vals[v // n, lax.rem(v, n) // 4, lax.rem(v, 4)].astype(F32)
        allv[:, pl.ds(v, 1), :] = tile[:GA][:, None, :]
        evm[pl.ds(v, 1), :] = tile[GA : GA + 1]
        return carry

    lax.fori_loop(0, nval, unfold, 0, unroll=8)
    index = lax.broadcasted_iota(jnp.int32, (nval, bc), 0).astype(F32)
    hot = []
    for t in range(pairs):
        one = jnp.where(index == hrecv[t : t + 1], 1.0, 0.0)
        hot.append(one.astype(BF16))
        e_v = jnp.sum(one * evm[...], axis=0, keepdims=True)
        slot = jnp.where(low1, 2.0 * t, 2.0 * t + 1.0)
        live = jnp.where(slot < hrecv[pairs + 16 : pairs + 17], 1.0, 0.0)
        for h in range(2):
            e_c = hrecv[pairs + 8 * h : pairs + 8 * h + 1]
            wrow[0:1, h * hcount + t * bc : h * hcount + (t + 1) * bc] = live * 2.0 / (e_c - e_v)
    hot = jnp.concatenate(hot, axis=1)

    def spread(a, carry):
        mult[pl.ds(pl.multiple_of(a * GB, GB), GB), :] = lax.dot_general(
            allv[a].astype(BF16), hot, (((0,), (0,)), ((), ())), preferred_element_type=F32
        ).astype(BF16)
        return carry

    lax.fori_loop(0, GA, spread, 0, unroll=8)

    for copy in tables:
        copy.wait()
    home_a = home_owner // per_a
    wide = min(2 * bc, hcount)

    for h in range(2):
        def do_first(step, carry):
            blocks = [
                lax.rem(home_a + GA - step * UNROLL_A[h] - r, GA) for r in range(UNROLL_A[h])
            ]
            for a in blocks:
                for q in range(per_a):
                    src = a * per_a + q
                    pltpu.make_async_copy(cblk.at[h, src], cblk.at[h, src], c_recv.at[h, src]).wait()
            for a in blocks:
                tops, bots = [], []
                for q in range(per_a):
                    part = cblk[h, a * per_a + q].astype(F32)
                    turn = pltpu.roll(part, hb, 1)
                    tops.append(jnp.where(low_c, part, turn))
                    tops.append(jnp.where(low_c, turn, part))
                block = jnp.concatenate(tops, axis=0).astype(BF16)
                block = jnp.concatenate([block] * (wide // bc), axis=1)
                for at in range(0, hcount, wide):
                    x = block * mult[pl.ds(pl.multiple_of(a * GB, GB), GB), at : at + wide]
                    f = jnp.dot(tb[...], x, preferred_element_type=F32).astype(BF16)
                    first[:, pl.ds(pl.multiple_of(a * rb, rb), rb), at : at + wide] = f.reshape(KG, rb, wide)
            return carry

        lax.fori_loop(0, GA // UNROLL_A[h], do_first, 0)

        def do_moved(kg, carry):
            start = pl.multiple_of(kg * rb, rb)
            for at in range(0, hcount, wide):
                sl = slice(h * hcount + at, h * hcount + at + wide)
                mv = jnp.dot(t2[...], first[kg, :, at : at + wide], preferred_element_type=F32).astype(BF16)
                for j in range(GA):
                    piece = mv[j * rb : (j + 1) * rb]
                    moved[pl.ds(j * GB + start, rb), sl] = piece
                    if j * GB < win:
                        wt[pl.ds(j * GB + start, rb), sl] = (piece.astype(F32) * wrow[0:1, sl]).astype(BF16)
            return carry

        lax.fori_loop(0, KG, do_moved, 0, unroll=True)

    mx, my = lax.rem(me, 2), lax.rem(me, 4) // 2
    px, py = 1 - mx, 1 - my
    x_peer = mz * 4 + my * 2 + px
    y_peer = mz * 4 + py * 2 + mx

    def target(i):
        return lax.rem(mz + 1 + i, groups)

    def step0(i):
        return remote(p0s.at[i], p0r.at[i], q0.at[i], r0.at[i], sibling, me)

    def step1(i):
        return [
            remote(s1a.at[i, 0], g1a.at[i, 0], q1.at[0, i], r1.at[0, i], my_ka, x_peer),
            remote(s1b.at[i, 0], g1b.at[i, 0], q1.at[1, i], r1.at[1, i], my_ka, y_peer),
            remote(s1a.at[i, 1], g1a.at[i, 1], q1.at[2, i], r1.at[2, i], my_ka, x_peer),
            remote(s1b.at[i, 1], g1b.at[i, 1], q1.at[3, i], r1.at[3, i], my_ka, y_peer),
        ]

    def step2(i):
        return [
            remote(s2a.at[i], g2a.at[i], q2.at[0, i], r2.at[0, i], my_ka, y_peer),
            remote(s2b.at[i], g2b.at[i], q2.at[1, i], r2.at[1, i], my_ka, x_peer),
        ]

    def step3(i):
        return remote(
            s3.at[i], g3.at[mz // 2, core], q3.at[i], r3.at[mz // 2, core],
            kb + zbit, target(i) * 4 + xy,
        )

    def product(i, side):
        z = target(i)
        return lax.dot_general(
            moved[pl.ds(pl.multiple_of(z * 4 * rows, 4 * rows), 4 * rows), :],
            wt[pl.ds(pl.multiple_of(side * half, half), half), :],
            (((1,), (1,)), ((), ())), preferred_element_type=F32,
        )

    def pair_sum(i, y, x, b):
        at = pl.ds(pl.multiple_of((2 * y + x) * rows, rows), rows)
        sl = slice(b * qw, (b + 1) * qw)
        return own[i, at, sl] + p0r[i, at, sl].astype(F32)

    def other_half(i):
        p0s[i] = product(i, 1 - core).astype(BF16)
        step0(i).start()

    def own_half(i):
        own[i] = product(i, core)

    def after0(i):
        step0(i).wait_recv()
        copies = step1(i)
        s1a[i, 0] = pair_sum(i, py, px, 0).astype(BF16)
        copies[0].start()
        s1b[i, 0] = pair_sum(i, py, px, 1).astype(BF16)
        copies[1].start()
        s1a[i, 1] = pair_sum(i, my, px, 0).astype(BF16)
        copies[2].start()
        s1b[i, 1] = pair_sum(i, py, mx, 1).astype(BF16)
        copies[3].start()

    def after1(i):
        first_copies, copies = step1(i), step2(i)
        first_copies[0].wait_recv()
        s2a[i] = (pair_sum(i, py, mx, 0) + g1a[i, 0].astype(F32)).astype(BF16)
        copies[0].start()
        first_copies[1].wait_recv()
        s2b[i] = (pair_sum(i, my, px, 1) + g1b[i, 0].astype(F32)).astype(BF16)
        copies[1].start()

    def after2(i):
        first_copies, second_copies = step1(i), step2(i)
        first_copies[2].wait_recv()
        first_copies[3].wait_recv()
        second_copies[0].wait_recv()
        a = pair_sum(i, my, mx, 0) + g1a[i, 1].astype(F32) + g2a[i].astype(F32)
        second_copies[1].wait_recv()
        b = pair_sum(i, my, mx, 1) + g1b[i, 1].astype(F32) + g2b[i].astype(F32)
        s3[i, :, :qw] = a.astype(BF16)
        s3[i, :, qw:] = b.astype(BF16)
        step3(i).start()

    last = groups - 1

    def direct(i):
        return remote(
            sd.at[i], gd.at[xy, core], qd.at[i], rd.at[xy, core], kb + zbit, mz * 4 + xor(xy, i, 4)
        )

    def finish():
        step0(last).wait_recv()
        for i in (3, 1, 2, 0):
            block = xor(xy, i, 4)
            at = pl.ds(pl.multiple_of(block * rows, rows), rows)
            total = (own[last, at] + p0r[last, at].astype(F32)).astype(BF16)
            if i > 0:
                sd[i] = total
                direct(i).start()
                continue

            @pl.when(at_home)
            def _():
                gd[xy, core] = total

            @pl.when(jnp.logical_not(at_home))
            def _():
                sd[0] = total
                direct(0).start()

    if groups == 4:
        order = (
            (other_half, 0), (own_half, 0), (other_half, 1), (after0, 0), (own_half, 1), (other_half, 2),
            (after0, 1), (own_half, 2), (other_half, 3), (after0, 2), (after1, 0), (own_half, 3), (finish, None),
            (after1, 1), (after2, 0), (after1, 2), (after2, 1), (after2, 2),
        )
        for stage, i in order:
            stage(*(() if i is None else (i,)))
    else:
        def flow(i, carry):
            for stage, lag in ((other_half, 0), (own_half, 0), (after0, 1), (after1, 3), (after2, 4)):
                @pl.when((i >= lag) & (i < last + lag))
                def _():
                    stage(i - lag)

            return carry

        lax.fori_loop(0, last + 4, flow, 0)
        other_half(last)
        own_half(last)
        finish()

    def arrived(w, q):
        pltpu.make_async_copy(g3.at[w, q], g3.at[w, q], r3.at[w, q]).wait()

    @pl.when(at_home)
    def _():
        for q in range(2):
            total = None
            for p in range(4):
                @pl.when((p != xy) | (q != core))
                def _():
                    pltpu.make_async_copy(gd.at[p, q], gd.at[p, q], rd.at[p, q]).wait()

                piece = gd[p, q].astype(F32)
                total = piece if total is None else total + piece
            for w in range(1, groups // 2):
                at = lax.rem(mz // 2 + w, groups // 2)
                arrived(at, q)
                total = total + g3[at, q].astype(F32)
            out_ref[:, q * half : (q + 1) * half] = total * scale

    @pl.when(jnp.logical_not(at_home))
    def _():
        for q in range(2):
            total = None
            for w in range(groups // 2):
                arrived(w, q)
                piece = g3[w, q].astype(F32)
                total = piece if total is None else total + piece
            out_ref[:, q * half : (q + 1) * half] = total * scale

    pltpu.make_async_copy(rest, rest, v_send).wait()
    for i in range(1, 4):
        plane_copy(i).wait_send()

    @pl.when(jnp.logical_not(at_home))
    def _():
        home_copy.wait_send()

    for h in range(2):
        @pl.when(jnp.logical_not(at_home))
        def _():
            cond_copy(h, me).wait_send()

        def drain_cond(i, carry):
            cond_copy(h, lax.rem(me + i, n)).wait_send()
            return carry

        lax.fori_loop(1, n, drain_cond, 0)

    def drain_lane(i, carry):
        lane_copy(i).wait_send()
        return carry

    lax.fori_loop(1, ka_size, drain_lane, 0)

    def drain(i, carry):
        for copy in [step0(i)] + step1(i) + step2(i) + [step3(i)]:
            copy.wait_send()
        return carry

    lax.fori_loop(0, last, drain, 0)
    step0(last).wait_send()
    for i in range(1, 4):
        direct(i).wait_send()

    @pl.when(jnp.logical_not(at_home))
    def _():
        direct(0).wait_send()


def shards(ka_size, n, cond_orbitals, cond_energy, val_orbitals, val_energy, val_slots, owner_count):
    cond = cond_orbitals[0]
    rows, bc = cond.shape[0], cond.shape[1] // n
    slots = val_slots.shape[2]
    win = 4 * GB
    half = win // 2
    grid = GA * GB
    count = slots * bc
    hcount = count // 2
    groups = n // 4
    nval = ka_size * n
    rb = GB // KG
    table_b = cosine_table(GB)
    table_2 = np.kron(cosine_table(GA), np.eye(rb, dtype=np.float32)).astype(jnp.bfloat16)
    scale = 2.0 / (slots * bc * n)
    vmem = pl.BlockSpec(memory_space=pltpu.VMEM)
    smem = pl.BlockSpec(memory_space=pltpu.SMEM)
    hbm = pl.BlockSpec(memory_space=pl.ANY)
    dma = pltpu.SemaphoreType.DMA
    out = pl.pallas_call(
        functools.partial(kernel, ka_size, n, scale),
        out_shape=pltpu.VMEM((rows, win), F32),
        in_specs=[smem, smem, vmem, vmem, vmem, hbm, hbm, hbm],
        out_specs=vmem,
        scratch_shapes=[
            pltpu.VMEM((GB, GB), BF16),
            pltpu.VMEM((GA * rb, GA * rb), BF16),
            pltpu.VMEM((rows, n * bc), BF16),
            pltpu.VMEM((2, n, rows // 2, bc), BF16),
            pltpu.VMEM((2, n, rows // 2, bc), BF16),
            pltpu.VMEM((GA + 8, GB), BF16),
            pltpu.VMEM((ka_size, groups, 4, GA + 8, GB), BF16),
            pltpu.VMEM((slots // 2 + 24, bc), F32),
            pltpu.VMEM((slots // 2 + 24, bc), F32),
            pltpu.VMEM((GA, nval, GB), F32),
            pltpu.VMEM((nval, GB), F32),
            pltpu.VMEM((grid, hcount), BF16),
            pltpu.VMEM((8, count), F32),
            pltpu.VMEM((KG, GA * rb, hcount), BF16),
            pltpu.VMEM((grid, count), BF16),
            pltpu.VMEM((win, count), BF16),
            pltpu.VMEM((groups, 4 * rows, half), F32),
            pltpu.VMEM((groups, 4 * rows, half), BF16),
            pltpu.VMEM((groups, 4 * rows, half), BF16),
            *[pltpu.VMEM((groups, 2, rows, half // 2), BF16)] * 4,
            *[pltpu.VMEM((groups, rows, half // 2), BF16)] * 4,
            pltpu.VMEM((groups, rows, half), BF16),
            pltpu.VMEM((groups // 2, 2, rows, half), BF16),
            pltpu.VMEM((4, rows, half), BF16),
            pltpu.VMEM((4, 2, rows, half), BF16),
            dma((2,)), dma(()), dma(()), dma(()), dma(()), dma((4,)), dma((4,)), dma((ka_size,)), dma((ka_size,)), dma(()), dma(()),
            dma((2, n)), dma((2, n)),
            dma((groups,)), dma((groups,)), dma((4, groups)), dma((4, groups)), dma((2, groups)), dma((2, groups)),
            dma((groups,)), dma((groups // 2, 2)), dma((4,)), dma((4, 2)),
        ],
        compiler_params=pltpu.CompilerParams(
            collective_id=0, has_side_effects=True, vmem_limit_bytes=60 * 1024 * 1024
        ),
        name="polarizability",
    )(
        val_slots[0, 0], owner_count[0], cond_energy, val_orbitals, val_energy[:, None],
        jnp.asarray(table_b), jnp.asarray(table_2), cond,
    )
    return out[None]


def solution(mesh):
    return jax.shard_map(
        functools.partial(shards, mesh.shape["ka"], mesh.shape["pair"]),
        mesh=mesh,
        in_specs=(
            P("ka", "pair", None),
            P("ka", "pair"),
            P(("ka", "pair"), None),
            P(("ka", "pair")),
            P("ka", "pair", None),
            P("ka", "pair"),
        ),
        out_specs=P("ka", "pair", None),
        check_vma=False,
    )
```

```python
import functools

import jax
import jax.numpy as jnp
import numpy as np
from jax import lax
from jax.experimental import pallas as pl
from jax.experimental.pallas import tpu as pltpu
from jax.sharding import PartitionSpec as P

GA = 16
GB = 128
KG = 8
UNROLL_A = (8, 8)
MESH = pl.DeviceIdType.MESH
F32 = jnp.float32
BF16 = jnp.bfloat16


def cosine_table(length):
    freq = np.arange(length, dtype=np.float32)[:, None]
    point = np.arange(length, dtype=np.float32)[None, :]
    factor = np.where(freq == 0, np.sqrt(np.float32(1.0 / length)), np.sqrt(np.float32(2.0 / length)))
    angle = np.float32(np.pi) * (point + np.float32(0.5)) * freq / np.float32(length)
    return (factor * np.cos(angle)).astype(jnp.bfloat16)


def xor(value, other, limit):
    out, bit = 0, 1
    while bit < limit:
        out = out + lax.rem(value // bit + other // bit, 2) * bit
        bit *= 2
    return out


def kernel(
    ka_size, n, scale,
    slots_ref, count_ref, ec_ref, row_ref, ev_ref, tb_hbm, t2_hbm, cond_hbm,
    out_ref,
    tb, t2, cond, csend, cblk, vmsg, vals, hmsg, hrecv, allv, evm, mult, wrow, first, moved, wt,
    own, p0s, p0r, s1a, s1b, g1a, g1b, s2a, s2b, g2a, g2b, s3, g3,
    t_sem, k_sem, v_own, v_send, v_recv, p_send, p_recv, l_send, l_recv, h_send, h_recv, c_send, c_recv,
    q0, r0, q1, r1, q2, r2, q3, r3,
):
    my_ka = lax.axis_index("ka")
    me = lax.axis_index("pair")
    core = lax.rem(my_ka, 2)
    kb = my_ka - core
    mz = me // 4
    xy = lax.rem(me, 4)
    zbit = lax.rem(mz, 2)
    sibling = kb + 1 - core
    slots = slots_ref.shape[0]
    bc = ec_ref.shape[1]
    hb = bc // 2
    pairs = slots // 2
    count = slots * bc
    hcount = count // 2
    rows = cond.shape[0]
    hr = rows // 2
    win = out_ref.shape[1]
    half = win // 2
    qw = half // 2
    groups = n // 4
    per_a = n // GA
    rb = GB // KG
    nval = ka_size * n
    home_owner = me + 4 * (core - zbit)
    at_home = core == zbit

    def remote(src, dst, ssem, rsem, ka, pair):
        return pltpu.make_async_remote_copy(
            src_ref=src, dst_ref=dst, send_sem=ssem, recv_sem=rsem,
            device_id=(ka, pair), device_id_type=MESH,
        )

    barrier = pltpu.get_barrier_semaphore()

    def greet(i, carry):
        other = lax.rem(me + i, n)
        for k in (my_ka, sibling):
            pl.semaphore_signal(barrier, inc=1, device_id=(k, other), device_id_type=MESH)
        return carry

    def greet_core(i, carry):
        pl.semaphore_signal(
            barrier, inc=1, device_id=(lax.rem(kb + i, ka_size), me), device_id_type=MESH
        )
        return carry

    cond_in = pltpu.make_async_copy(cond_hbm, cond, k_sem)
    cond_in.start()
    lax.fori_loop(1, n, greet, 0)
    pl.semaphore_signal(barrier, inc=1, device_id=(sibling, me), device_id_type=MESH)
    lax.fori_loop(2, ka_size, greet_core, 0)
    tables = (pltpu.make_async_copy(tb_hbm, tb, t_sem.at[0]), pltpu.make_async_copy(t2_hbm, t2, t_sem.at[1]))
    for copy in tables:
        copy.start()

    row = row_ref[...].astype(F32)
    grid_rows = [row[:, a * GB : (a + 1) * GB] for a in range(GA)]
    energy = jnp.broadcast_to(ev_ref[...].astype(F32), (8, GB))
    vmsg[...] = jnp.concatenate(grid_rows + [energy], axis=0).astype(BF16)
    own_val = pltpu.make_async_copy(vmsg, vals.at[my_ka, mz, xy], v_own)
    own_val.start()

    low = lax.broadcasted_iota(jnp.int32, (8, bc), 1) < hb
    low1 = lax.broadcasted_iota(jnp.int32, (1, bc), 1) < hb
    for t in range(pairs):
        hmsg[t : t + 1] = jnp.where(low1, slots_ref[2 * t], slots_ref[2 * t + 1]).astype(F32)
    ec = jnp.broadcast_to(ec_ref[...], (8, bc))
    turned = pltpu.roll(ec, hb, 1)
    hmsg[pairs : pairs + 8] = jnp.where(low, ec, turned)
    hmsg[pairs + 8 : pairs + 16] = jnp.where(low, turned, ec)
    hmsg[pairs + 16 : pairs + 24] = jnp.broadcast_to(count_ref[0], (8, bc)).astype(F32)

    cond_in.wait()
    low_c = lax.broadcasted_iota(jnp.int32, (hr, bc), 1) < hb

    def pack(o, carry):
        block = cond[:, pl.ds(pl.multiple_of(o * bc, bc), bc)].astype(F32)
        top, bot = block[:hr], block[hr:]
        csend[0, o] = jnp.where(low_c, top, pltpu.roll(bot, hb, 1)).astype(BF16)
        csend[1, o] = jnp.where(low_c, pltpu.roll(top, hb, 1), bot).astype(BF16)
        return carry

    lax.fori_loop(0, n, pack, 0, unroll=4)
    own_val.wait()

    pl.semaphore_wait(barrier, 2 * n - 1 + ka_size - 2)

    def send_val(i, carry):
        remote(
            vmsg, vals.at[my_ka, mz, xy], v_send, v_recv, my_ka, lax.rem(mz + i, groups) * 4 + xy
        ).start()
        return carry

    lax.fori_loop(1, groups, send_val, 0)
    column = vals.at[my_ka, pl.ds(0, groups), xy]
    rest = vals.at[my_ka, pl.ds(0, groups - 1), xy]

    def plane_copy(i):
        return remote(column, column, p_send.at[i], p_recv.at[i], my_ka, mz * 4 + xor(xy, i, 4))

    home_copy = remote(hmsg, hrecv, h_send, h_recv, sibling, home_owner)

    @pl.when(at_home)
    def _():
        hrecv[...] = hmsg[...]

    @pl.when(jnp.logical_not(at_home))
    def _():
        home_copy.start()

    def cond_copy(h, o):
        obit = lax.rem(o // 4, 2)
        return remote(
            csend.at[h, o], cblk.at[h, me], c_send.at[h, o], c_recv.at[h, me],
            kb + obit, o + 4 * (core - obit),
        )

    def own_cond(h):
        return pltpu.make_async_copy(csend.at[h, me], cblk.at[h, me], c_recv.at[h, me])

    def send_low(h):
        @pl.when(at_home)
        def _():
            own_cond(h).start()

        @pl.when(jnp.logical_not(at_home))
        def _():
            cond_copy(h, me).start()

        lax.fori_loop(1, n // 2, functools.partial(send_cond, h), 0)

    def send_cond(h, i, carry):
        cond_copy(h, lax.rem(me + i, n)).start()
        return carry

    def send_high(h):
        lax.fori_loop(n // 2, n, functools.partial(send_cond, h), 0)

    send_low(0)
    send_high(0)
    pltpu.make_async_copy(rest, rest, v_recv).wait()
    for i in range(1, 4):
        plane_copy(i).start()
    send_low(1)
    send_high(1)
    for i in range(1, 4):
        peer = vals.at[my_ka, pl.ds(0, groups), xor(xy, i, 4)]
        pltpu.make_async_copy(peer, peer, p_recv.at[i]).wait()

    def lane_copy(i):
        other = lax.rem(my_ka + i, ka_size)
        return remote(vals.at[my_ka], vals.at[my_ka], l_send.at[other], l_recv.at[my_ka], other, me)

    def send_lane(i, carry):
        lane_copy(i).start()
        return carry

    def wait_lane(i, carry):
        other = lax.rem(my_ka + i, ka_size)
        pltpu.make_async_copy(vals.at[other], vals.at[other], l_recv.at[other]).wait()
        return carry

    lax.fori_loop(1, ka_size, send_lane, 0)
    lax.fori_loop(1, ka_size, wait_lane, 0)

    @pl.when(jnp.logical_not(at_home))
    def _():
        home_copy.wait_recv()

    def unfold(v, carry):
        tile = vals[v // n, lax.rem(v, n) // 4, lax.rem(v, 4)].astype(F32)
        allv[:, pl.ds(v, 1), :] = tile[:GA][:, None, :]
        evm[pl.ds(v, 1), :] = tile[GA : GA + 1]
        return carry

    lax.fori_loop(0, nval, unfold, 0, unroll=8)
    index = lax.broadcasted_iota(jnp.int32, (nval, bc), 0).astype(F32)
    hot = []
    for t in range(pairs):
        one = jnp.where(index == hrecv[t : t + 1], 1.0, 0.0)
        hot.append(one.astype(BF16))
        e_v = jnp.sum(one * evm[...], axis=0, keepdims=True)
        slot = jnp.where(low1, 2.0 * t, 2.0 * t + 1.0)
        live = jnp.where(slot < hrecv[pairs + 16 : pairs + 17], 1.0, 0.0)
        for h in range(2):
            e_c = hrecv[pairs + 8 * h : pairs + 8 * h + 1]
            wrow[0:1, h * hcount + t * bc : h * hcount + (t + 1) * bc] = live * 2.0 / (e_c - e_v)
    hot = jnp.concatenate(hot, axis=1)

    def spread(a, carry):
        mult[pl.ds(pl.multiple_of(a * GB, GB), GB), :] = lax.dot_general(
            allv[a].astype(BF16), hot, (((0,), (0,)), ((), ())), preferred_element_type=F32
        ).astype(BF16)
        return carry

    lax.fori_loop(0, GA, spread, 0, unroll=8)

    for copy in tables:
        copy.wait()
    home_a = home_owner // per_a
    wide = min(2 * bc, hcount)

    for h in range(2):
        def do_first(step, carry):
            blocks = [
                lax.rem(home_a + GA - step * UNROLL_A[h] - r, GA) for r in range(UNROLL_A[h])
            ]
            for a in blocks:
                for q in range(per_a):
                    src = a * per_a + q
                    pltpu.make_async_copy(cblk.at[h, src], cblk.at[h, src], c_recv.at[h, src]).wait()
            for a in blocks:
                tops, bots = [], []
                for q in range(per_a):
                    part = cblk[h, a * per_a + q].astype(F32)
                    turn = pltpu.roll(part, hb, 1)
                    tops.append(jnp.where(low_c, part, turn))
                    tops.append(jnp.where(low_c, turn, part))
                block = jnp.concatenate(tops, axis=0).astype(BF16)
                block = jnp.concatenate([block] * (wide // bc), axis=1)
                for at in range(0, hcount, wide):
                    x = block * mult[pl.ds(pl.multiple_of(a * GB, GB), GB), at : at + wide]
                    f = jnp.dot(tb[...], x, preferred_element_type=F32).astype(BF16)
                    first[:, pl.ds(pl.multiple_of(a * rb, rb), rb), at : at + wide] = f.reshape(KG, rb, wide)
            return carry

        lax.fori_loop(0, GA // UNROLL_A[h], do_first, 0)

        def do_moved(kg, carry):
            start = pl.multiple_of(kg * rb, rb)
            for at in range(0, hcount, wide):
                sl = slice(h * hcount + at, h * hcount + at + wide)
                mv = jnp.dot(t2[...], first[kg, :, at : at + wide], preferred_element_type=F32).astype(BF16)
                for j in range(GA):
                    piece = mv[j * rb : (j + 1) * rb]
                    moved[pl.ds(j * GB + start, rb), sl] = piece
                    if j * GB < win:
                        wt[pl.ds(j * GB + start, rb), sl] = (piece.astype(F32) * wrow[0:1, sl]).astype(BF16)
            return carry

        lax.fori_loop(0, KG, do_moved, 0, unroll=True)

    mx, my = lax.rem(me, 2), lax.rem(me, 4) // 2
    px, py = 1 - mx, 1 - my
    x_peer = mz * 4 + my * 2 + px
    y_peer = mz * 4 + py * 2 + mx

    def target(i):
        return xor(mz, groups - 1 - i, groups)

    def step0(i):
        return remote(p0s.at[i], p0r.at[i], q0.at[i], r0.at[i], sibling, me)

    def step1(i):
        return [
            remote(s1a.at[i, 0], g1a.at[i, 0], q1.at[0, i], r1.at[0, i], my_ka, x_peer),
            remote(s1b.at[i, 0], g1b.at[i, 0], q1.at[1, i], r1.at[1, i], my_ka, y_peer),
            remote(s1a.at[i, 1], g1a.at[i, 1], q1.at[2, i], r1.at[2, i], my_ka, x_peer),
            remote(s1b.at[i, 1], g1b.at[i, 1], q1.at[3, i], r1.at[3, i], my_ka, y_peer),
        ]

    def step2(i):
        return [
            remote(s2a.at[i], g2a.at[i], q2.at[0, i], r2.at[0, i], my_ka, y_peer),
            remote(s2b.at[i], g2b.at[i], q2.at[1, i], r2.at[1, i], my_ka, x_peer),
        ]

    def step3(i):
        return remote(
            s3.at[i], g3.at[mz // 2, core], q3.at[i], r3.at[mz // 2, core],
            kb + zbit, target(i) * 4 + xy,
        )

    def product(i, side):
        z = target(i)
        return lax.dot_general(
            moved[pl.ds(pl.multiple_of(z * 4 * rows, 4 * rows), 4 * rows), :],
            wt[pl.ds(pl.multiple_of(side * half, half), half), :],
            (((1,), (1,)), ((), ())), preferred_element_type=F32,
        )

    def pair_sum(i, y, x, b):
        at = pl.ds(pl.multiple_of((2 * y + x) * rows, rows), rows)
        sl = slice(b * qw, (b + 1) * qw)
        return own[i, at, sl] + p0r[i, at, sl].astype(F32)

    def other_half(i):
        p0s[i] = product(i, 1 - core).astype(BF16)
        step0(i).start()

    def own_half(i):
        own[i] = product(i, core)

    def after0(i):
        step0(i).wait_recv()
        copies = step1(i)
        s1a[i, 0] = pair_sum(i, py, px, 0).astype(BF16)
        copies[0].start()
        s1b[i, 0] = pair_sum(i, py, px, 1).astype(BF16)
        copies[1].start()

    def rest0(i):
        copies = step1(i)
        s1a[i, 1] = pair_sum(i, my, px, 0).astype(BF16)
        copies[2].start()
        s1b[i, 1] = pair_sum(i, py, mx, 1).astype(BF16)
        copies[3].start()

    def after1(i):
        first_copies, copies = step1(i), step2(i)
        first_copies[0].wait_recv()
        s2a[i] = (pair_sum(i, py, mx, 0) + g1a[i, 0].astype(F32)).astype(BF16)
        copies[0].start()
        first_copies[1].wait_recv()
        s2b[i] = (pair_sum(i, my, px, 1) + g1b[i, 0].astype(F32)).astype(BF16)
        copies[1].start()

    def after2(i):
        first_copies, second_copies = step1(i), step2(i)
        first_copies[2].wait_recv()
        first_copies[3].wait_recv()
        second_copies[0].wait_recv()
        a = pair_sum(i, my, mx, 0) + g1a[i, 1].astype(F32) + g2a[i].astype(F32)
        second_copies[1].wait_recv()
        b = pair_sum(i, my, mx, 1) + g1b[i, 1].astype(F32) + g2b[i].astype(F32)
        a, b = a.astype(BF16), b.astype(BF16)
        stays = at_home & (i == groups - 1)

        @pl.when(stays)
        def _():
            g3[mz // 2, core, :, :qw] = a
            g3[mz // 2, core, :, qw:] = b

        @pl.when(jnp.logical_not(stays))
        def _():
            s3[i, :, :qw] = a
            s3[i, :, qw:] = b
            step3(i).start()

    if groups == 4:
        order = (
            (other_half, 0), (own_half, 0), (other_half, 1), (after0, 0), (rest0, 0), (own_half, 1), (other_half, 2),
            (after0, 1), (rest0, 1), (own_half, 2), (other_half, 3), (after0, 2), (after1, 0), (own_half, 3), (after0, 3),
            (rest0, 2), (after1, 1), (after1, 2), (rest0, 3), (after2, 0), (after1, 3), (after2, 1), (after2, 2), (after2, 3),
        )
        for stage, i in order:
            stage(i)
    else:
        def flow(i, carry):
            for stage, lag in ((other_half, 0), (own_half, 0), (after0, 1), (rest0, 1), (after1, 3), (after2, 4)):
                @pl.when((i >= lag) & (i < groups + lag))
                def _():
                    stage(i - lag)

            return carry

        lax.fori_loop(0, groups + 4, flow, 0)

    for q in range(2):
        for w in range(groups // 2):
            mine = at_home & (w == mz // 2) & (q == core)

            @pl.when(jnp.logical_not(mine))
            def _():
                pltpu.make_async_copy(g3.at[w, q], g3.at[w, q], r3.at[w, q]).wait()

        total = g3[0, q].astype(F32)
        for w in range(1, groups // 2):
            total = total + g3[w, q].astype(F32)
        out_ref[:, q * half : (q + 1) * half] = total * scale

    pltpu.make_async_copy(rest, rest, v_send).wait()
    for i in range(1, 4):
        plane_copy(i).wait_send()

    @pl.when(jnp.logical_not(at_home))
    def _():
        home_copy.wait_send()

    for h in range(2):
        @pl.when(jnp.logical_not(at_home))
        def _():
            cond_copy(h, me).wait_send()

        def drain_cond(i, carry):
            cond_copy(h, lax.rem(me + i, n)).wait_send()
            return carry

        lax.fori_loop(1, n, drain_cond, 0)

    def drain_lane(i, carry):
        lane_copy(i).wait_send()
        return carry

    lax.fori_loop(1, ka_size, drain_lane, 0)

    def drain(i, carry):
        for copy in [step0(i)] + step1(i) + step2(i):
            copy.wait_send()

        @pl.when(jnp.logical_not(at_home & (i == groups - 1)))
        def _():
            step3(i).wait_send()

        return carry

    lax.fori_loop(0, groups, drain, 0)


def shards(ka_size, n, cond_orbitals, cond_energy, val_orbitals, val_energy, val_slots, owner_count):
    cond = cond_orbitals[0]
    rows, bc = cond.shape[0], cond.shape[1] // n
    slots = val_slots.shape[2]
    win = 4 * GB
    half = win // 2
    grid = GA * GB
    count = slots * bc
    hcount = count // 2
    groups = n // 4
    nval = ka_size * n
    rb = GB // KG
    table_b = cosine_table(GB)
    table_2 = np.kron(cosine_table(GA), np.eye(rb, dtype=np.float32)).astype(jnp.bfloat16)
    scale = 2.0 / (slots * bc * n)
    vmem = pl.BlockSpec(memory_space=pltpu.VMEM)
    smem = pl.BlockSpec(memory_space=pltpu.SMEM)
    hbm = pl.BlockSpec(memory_space=pl.ANY)
    dma = pltpu.SemaphoreType.DMA
    out = pl.pallas_call(
        functools.partial(kernel, ka_size, n, scale),
        out_shape=pltpu.VMEM((rows, win), F32),
        in_specs=[smem, smem, vmem, vmem, vmem, hbm, hbm, hbm],
        out_specs=vmem,
        scratch_shapes=[
            pltpu.VMEM((GB, GB), BF16),
            pltpu.VMEM((GA * rb, GA * rb), BF16),
            pltpu.VMEM((rows, n * bc), BF16),
            pltpu.VMEM((2, n, rows // 2, bc), BF16),
            pltpu.VMEM((2, n, rows // 2, bc), BF16),
            pltpu.VMEM((GA + 8, GB), BF16),
            pltpu.VMEM((ka_size, groups, 4, GA + 8, GB), BF16),
            pltpu.VMEM((slots // 2 + 24, bc), F32),
            pltpu.VMEM((slots // 2 + 24, bc), F32),
            pltpu.VMEM((GA, nval, GB), F32),
            pltpu.VMEM((nval, GB), F32),
            pltpu.VMEM((grid, hcount), BF16),
            pltpu.VMEM((8, count), F32),
            pltpu.VMEM((KG, GA * rb, hcount), BF16),
            pltpu.VMEM((grid, count), BF16),
            pltpu.VMEM((win, count), BF16),
            pltpu.VMEM((groups, 4 * rows, half), F32),
            pltpu.VMEM((groups, 4 * rows, half), BF16),
            pltpu.VMEM((groups, 4 * rows, half), BF16),
            *[pltpu.VMEM((groups, 2, rows, half // 2), BF16)] * 4,
            *[pltpu.VMEM((groups, rows, half // 2), BF16)] * 4,
            pltpu.VMEM((groups, rows, half), BF16),
            pltpu.VMEM((groups // 2, 2, rows, half), BF16),
            dma((2,)), dma(()), dma(()), dma(()), dma(()), dma((4,)), dma((4,)), dma((ka_size,)), dma((ka_size,)), dma(()), dma(()),
            dma((2, n)), dma((2, n)),
            dma((groups,)), dma((groups,)), dma((4, groups)), dma((4, groups)), dma((2, groups)), dma((2, groups)),
            dma((groups,)), dma((groups // 2, 2)),
        ],
        compiler_params=pltpu.CompilerParams(
            collective_id=0, has_side_effects=True, vmem_limit_bytes=60 * 1024 * 1024
        ),
        name="polarizability",
    )(
        val_slots[0, 0], owner_count[0], cond_energy, val_orbitals, val_energy[:, None],
        jnp.asarray(table_b), jnp.asarray(table_2), cond,
    )
    return out[None]


def solution(mesh):
    return jax.shard_map(
        functools.partial(shards, mesh.shape["ka"], mesh.shape["pair"]),
        mesh=mesh,
        in_specs=(
            P("ka", "pair", None),
            P("ka", "pair"),
            P(("ka", "pair"), None),
            P(("ka", "pair")),
            P("ka", "pair", None),
            P("ka", "pair"),
        ),
        out_specs=P("ka", "pair", None),
        check_vma=False,
    )
```

```python
import functools

import jax
import jax.numpy as jnp
import numpy as np
from jax import lax
from jax.experimental import pallas as pl
from jax.experimental.pallas import tpu as pltpu
from jax.sharding import PartitionSpec as P

GA = 16
GB = 128
KG = 8
UNROLL_A = (8, 8)
MESH = pl.DeviceIdType.MESH
F32 = jnp.float32
BF16 = jnp.bfloat16


def cosine_table(length):
    freq = np.arange(length, dtype=np.float32)[:, None]
    point = np.arange(length, dtype=np.float32)[None, :]
    factor = np.where(freq == 0, np.sqrt(np.float32(1.0 / length)), np.sqrt(np.float32(2.0 / length)))
    angle = np.float32(np.pi) * (point + np.float32(0.5)) * freq / np.float32(length)
    return (factor * np.cos(angle)).astype(jnp.bfloat16)


def xor(value, other, limit):
    out, bit = 0, 1
    while bit < limit:
        out = out + lax.rem(value // bit + other // bit, 2) * bit
        bit *= 2
    return out


def kernel(
    ka_size, n, scale,
    slots_hbm, count_hbm, ec_hbm, row_hbm, ev_hbm, tb_hbm, t2_hbm, cond_hbm,
    out_ref,
    slots_ref, count_ref, ec_ref, row_ref, ev_ref, tb, t2, cond, csend, cblk, vmsg, vals, hmsg, hrecv, allv, evm, mult, wrow, first, moved, wt,
    own, p0s, p0r, s1a, s1b, g1a, g1b, s2a, s2b, g2a, g2b, s3, g3,
    e_sem, t_sem, k_sem, v_own, v_send, v_recv, p_send, p_recv, l_send, l_recv, h_send, h_recv, c_send, c_recv,
    q0, r0, q1, r1, q2, r2, q3, r3,
):
    my_ka = lax.axis_index("ka")
    me = lax.axis_index("pair")
    core = lax.rem(my_ka, 2)
    kb = my_ka - core
    mz = me // 4
    xy = lax.rem(me, 4)
    zbit = lax.rem(mz, 2)
    sibling = kb + 1 - core
    slots = slots_ref.shape[0]
    bc = ec_ref.shape[1]
    hb = bc // 2
    pairs = slots // 2
    count = slots * bc
    hcount = count // 2
    rows = cond.shape[0]
    hr = rows // 2
    win = out_ref.shape[1]
    half = win // 2
    qw = half // 2
    groups = n // 4
    per_a = n // GA
    rb = GB // KG
    nval = ka_size * n
    home_owner = me + 4 * (core - zbit)
    at_home = core == zbit

    def remote(src, dst, ssem, rsem, ka, pair):
        return pltpu.make_async_remote_copy(
            src_ref=src, dst_ref=dst, send_sem=ssem, recv_sem=rsem,
            device_id=(ka, pair), device_id_type=MESH,
        )

    barrier = pltpu.get_barrier_semaphore()

    def greet(i, carry):
        other = lax.rem(me + i, n)
        for k in (my_ka, sibling):
            pl.semaphore_signal(barrier, inc=1, device_id=(k, other), device_id_type=MESH)
        return carry

    def greet_core(i, carry):
        pl.semaphore_signal(
            barrier, inc=1, device_id=(lax.rem(kb + i, ka_size), me), device_id_type=MESH
        )
        return carry

    cond_in = pltpu.make_async_copy(cond_hbm, cond, k_sem)
    lax.fori_loop(1, n, greet, 0)
    pl.semaphore_signal(barrier, inc=1, device_id=(sibling, me), device_id_type=MESH)
    lax.fori_loop(2, ka_size, greet_core, 0)
    small = [
        pltpu.make_async_copy(src, dst, e_sem.at[i])
        for i, (src, dst) in enumerate((
            (slots_hbm, slots_ref), (count_hbm, count_ref), (ec_hbm, ec_ref), (row_hbm, row_ref), (ev_hbm, ev_ref),
        ))
    ]
    for copy in small:
        copy.start()
    cond_in.start()
    tables = (pltpu.make_async_copy(tb_hbm, tb, t_sem.at[0]), pltpu.make_async_copy(t2_hbm, t2, t_sem.at[1]))
    for copy in tables:
        copy.start()

    for copy in small:
        copy.wait()

    row = row_ref[...].astype(F32)
    grid_rows = [row[:, a * GB : (a + 1) * GB] for a in range(GA)]
    energy = jnp.broadcast_to(ev_ref[0].astype(F32), (8, GB))
    vmsg[...] = jnp.concatenate(grid_rows + [energy], axis=0).astype(BF16)
    own_val = pltpu.make_async_copy(vmsg, vals.at[my_ka, mz, xy], v_own)
    own_val.start()

    low = lax.broadcasted_iota(jnp.int32, (8, bc), 1) < hb
    low1 = lax.broadcasted_iota(jnp.int32, (1, bc), 1) < hb
    for t in range(pairs):
        hmsg[t : t + 1] = jnp.where(low1, slots_ref[2 * t], slots_ref[2 * t + 1]).astype(F32)
    ec = jnp.broadcast_to(ec_ref[...], (8, bc))
    turned = pltpu.roll(ec, hb, 1)
    hmsg[pairs : pairs + 8] = jnp.where(low, ec, turned)
    hmsg[pairs + 8 : pairs + 16] = jnp.where(low, turned, ec)
    hmsg[pairs + 16 : pairs + 24] = jnp.broadcast_to(count_ref[0, 0], (8, bc)).astype(F32)

    cond_in.wait()
    low_c = lax.broadcasted_iota(jnp.int32, (hr, bc), 1) < hb

    def pack(o, carry):
        block = cond[:, pl.ds(pl.multiple_of(o * bc, bc), bc)].astype(F32)
        top, bot = block[:hr], block[hr:]
        csend[0, o] = jnp.where(low_c, top, pltpu.roll(bot, hb, 1)).astype(BF16)
        csend[1, o] = jnp.where(low_c, pltpu.roll(top, hb, 1), bot).astype(BF16)
        return carry

    lax.fori_loop(0, n, pack, 0, unroll=4)
    own_val.wait()

    pl.semaphore_wait(barrier, 2 * n - 1 + ka_size - 2)

    def send_val(i, carry):
        remote(
            vmsg, vals.at[my_ka, mz, xy], v_send, v_recv, my_ka, lax.rem(mz + i, groups) * 4 + xy
        ).start()
        return carry

    lax.fori_loop(1, groups, send_val, 0)
    column = vals.at[my_ka, pl.ds(0, groups), xy]
    rest = vals.at[my_ka, pl.ds(0, groups - 1), xy]

    def plane_copy(i):
        return remote(column, column, p_send.at[i], p_recv.at[i], my_ka, mz * 4 + xor(xy, i, 4))

    home_copy = remote(hmsg, hrecv, h_send, h_recv, sibling, home_owner)

    @pl.when(at_home)
    def _():
        hrecv[...] = hmsg[...]

    @pl.when(jnp.logical_not(at_home))
    def _():
        home_copy.start()

    def cond_copy(h, o):
        obit = lax.rem(o // 4, 2)
        return remote(
            csend.at[h, o], cblk.at[h, me], c_send.at[h, o], c_recv.at[h, me],
            kb + obit, o + 4 * (core - obit),
        )

    def own_cond(h):
        return pltpu.make_async_copy(csend.at[h, me], cblk.at[h, me], c_recv.at[h, me])

    def send_low(h):
        @pl.when(at_home)
        def _():
            own_cond(h).start()

        @pl.when(jnp.logical_not(at_home))
        def _():
            cond_copy(h, me).start()

        lax.fori_loop(1, n // 2, functools.partial(send_cond, h), 0)

    def send_cond(h, i, carry):
        cond_copy(h, lax.rem(me + i, n)).start()
        return carry

    def send_high(h):
        lax.fori_loop(n // 2, n, functools.partial(send_cond, h), 0)

    send_low(0)
    send_high(0)
    pltpu.make_async_copy(rest, rest, v_recv).wait()
    for i in range(1, 4):
        plane_copy(i).start()
    send_low(1)
    for i in range(1, 4):
        peer = vals.at[my_ka, pl.ds(0, groups), xor(xy, i, 4)]
        pltpu.make_async_copy(peer, peer, p_recv.at[i]).wait()

    def lane_copy(i):
        other = lax.rem(my_ka + i, ka_size)
        return remote(vals.at[my_ka], vals.at[my_ka], l_send.at[other], l_recv.at[my_ka], other, me)

    def send_lane(i, carry):
        lane_copy(i).start()
        return carry

    def wait_lane(i, carry):
        other = lax.rem(my_ka + i, ka_size)
        pltpu.make_async_copy(vals.at[other], vals.at[other], l_recv.at[other]).wait()
        return carry

    lax.fori_loop(1, ka_size, send_lane, 0)
    lax.fori_loop(1, ka_size, wait_lane, 0)
    send_high(1)

    @pl.when(jnp.logical_not(at_home))
    def _():
        home_copy.wait_recv()

    def unfold(v, carry):
        tile = vals[v // n, lax.rem(v, n) // 4, lax.rem(v, 4)].astype(F32)
        allv[:, pl.ds(v, 1), :] = tile[:GA][:, None, :]
        evm[pl.ds(v, 1), :] = tile[GA : GA + 1]
        return carry

    lax.fori_loop(0, nval, unfold, 0, unroll=8)
    index = lax.broadcasted_iota(jnp.int32, (nval, bc), 0).astype(F32)
    hot = []
    for t in range(pairs):
        one = jnp.where(index == hrecv[t : t + 1], 1.0, 0.0)
        hot.append(one.astype(BF16))
        e_v = jnp.sum(one * evm[...], axis=0, keepdims=True)
        slot = jnp.where(low1, 2.0 * t, 2.0 * t + 1.0)
        live = jnp.where(slot < hrecv[pairs + 16 : pairs + 17], 1.0, 0.0)
        for h in range(2):
            e_c = hrecv[pairs + 8 * h : pairs + 8 * h + 1]
            wrow[0:1, h * hcount + t * bc : h * hcount + (t + 1) * bc] = live * 2.0 / (e_c - e_v)
    hot = jnp.concatenate(hot, axis=1)

    def spread(a, carry):
        mult[pl.ds(pl.multiple_of(a * GB, GB), GB), :] = lax.dot_general(
            allv[a].astype(BF16), hot, (((0,), (0,)), ((), ())), preferred_element_type=F32
        ).astype(BF16)
        return carry

    lax.fori_loop(0, GA, spread, 0, unroll=8)

    for copy in tables:
        copy.wait()
    home_a = home_owner // per_a
    wide = min(2 * bc, hcount)

    for h in range(2):
        def do_first(step, carry):
            blocks = [
                lax.rem(home_a + GA - step * UNROLL_A[h] - r, GA) for r in range(UNROLL_A[h])
            ]
            for a in blocks:
                for q in range(per_a):
                    src = a * per_a + q
                    pltpu.make_async_copy(cblk.at[h, src], cblk.at[h, src], c_recv.at[h, src]).wait()
            for a in blocks:
                tops, bots = [], []
                for q in range(per_a):
                    part = cblk[h, a * per_a + q].astype(F32)
                    turn = pltpu.roll(part, hb, 1)
                    tops.append(jnp.where(low_c, part, turn))
                    tops.append(jnp.where(low_c, turn, part))
                block = jnp.concatenate(tops, axis=0).astype(BF16)
                block = jnp.concatenate([block] * (wide // bc), axis=1)
                for at in range(0, hcount, wide):
                    x = block * mult[pl.ds(pl.multiple_of(a * GB, GB), GB), at : at + wide]
                    f = jnp.dot(tb[...], x, preferred_element_type=F32).astype(BF16)
                    first[:, pl.ds(pl.multiple_of(a * rb, rb), rb), at : at + wide] = f.reshape(KG, rb, wide)
            return carry

        lax.fori_loop(0, GA // UNROLL_A[h], do_first, 0)

        def do_moved(kg, carry):
            start = pl.multiple_of(kg * rb, rb)
            for at in range(0, hcount, wide):
                sl = slice(h * hcount + at, h * hcount + at + wide)
                mv = jnp.dot(t2[...], first[kg, :, at : at + wide], preferred_element_type=F32).astype(BF16)
                for j in range(GA):
                    piece = mv[j * rb : (j + 1) * rb]
                    moved[pl.ds(j * GB + start, rb), sl] = piece
                    if j * GB < win:
                        wt[pl.ds(j * GB + start, rb), sl] = (piece.astype(F32) * wrow[0:1, sl]).astype(BF16)
            return carry

        lax.fori_loop(0, KG, do_moved, 0, unroll=True)

    mx, my = lax.rem(me, 2), lax.rem(me, 4) // 2
    px, py = 1 - mx, 1 - my
    x_peer = mz * 4 + my * 2 + px
    y_peer = mz * 4 + py * 2 + mx

    def target(i):
        return xor(mz, groups - 1 - i, groups)

    def step0(i):
        return remote(p0s.at[i], p0r.at[i], q0.at[i], r0.at[i], sibling, me)

    def step1(i):
        return [
            remote(s1a.at[i, 0], g1a.at[i, 0], q1.at[0, i], r1.at[0, i], my_ka, x_peer),
            remote(s1b.at[i, 0], g1b.at[i, 0], q1.at[1, i], r1.at[1, i], my_ka, y_peer),
            remote(s1a.at[i, 1], g1a.at[i, 1], q1.at[2, i], r1.at[2, i], my_ka, x_peer),
            remote(s1b.at[i, 1], g1b.at[i, 1], q1.at[3, i], r1.at[3, i], my_ka, y_peer),
        ]

    def step2(i):
        return [
            remote(s2a.at[i], g2a.at[i], q2.at[0, i], r2.at[0, i], my_ka, y_peer),
            remote(s2b.at[i], g2b.at[i], q2.at[1, i], r2.at[1, i], my_ka, x_peer),
        ]

    def step3(i):
        return remote(
            s3.at[i], g3.at[mz // 2, core], q3.at[i], r3.at[mz // 2, core],
            kb + zbit, target(i) * 4 + xy,
        )

    def product(i, side):
        z = target(i)
        return lax.dot_general(
            moved[pl.ds(pl.multiple_of(z * 4 * rows, 4 * rows), 4 * rows), :],
            wt[pl.ds(pl.multiple_of(side * half, half), half), :],
            (((1,), (1,)), ((), ())), preferred_element_type=F32,
        )

    def pair_sum(i, y, x, b):
        at = pl.ds(pl.multiple_of((2 * y + x) * rows, rows), rows)
        sl = slice(b * qw, (b + 1) * qw)
        return own[i, at, sl] + p0r[i, at, sl].astype(F32)

    def other_half(i):
        p0s[i] = product(i, 1 - core).astype(BF16)
        step0(i).start()

    def own_half(i):
        own[i] = product(i, core)

    def after0(i):
        step0(i).wait_recv()
        copies = step1(i)
        s1a[i, 0] = pair_sum(i, py, px, 0).astype(BF16)
        copies[0].start()
        s1b[i, 0] = pair_sum(i, py, px, 1).astype(BF16)
        copies[1].start()

    def rest0(i):
        copies = step1(i)
        s1a[i, 1] = pair_sum(i, my, px, 0).astype(BF16)
        copies[2].start()
        s1b[i, 1] = pair_sum(i, py, mx, 1).astype(BF16)
        copies[3].start()

    def after1(i):
        first_copies, copies = step1(i), step2(i)
        first_copies[0].wait_recv()
        s2a[i] = (pair_sum(i, py, mx, 0) + g1a[i, 0].astype(F32)).astype(BF16)
        copies[0].start()
        first_copies[1].wait_recv()
        s2b[i] = (pair_sum(i, my, px, 1) + g1b[i, 0].astype(F32)).astype(BF16)
        copies[1].start()

    def after2(i):
        first_copies, second_copies = step1(i), step2(i)
        first_copies[2].wait_recv()
        first_copies[3].wait_recv()
        second_copies[0].wait_recv()
        a = pair_sum(i, my, mx, 0) + g1a[i, 1].astype(F32) + g2a[i].astype(F32)
        second_copies[1].wait_recv()
        b = pair_sum(i, my, mx, 1) + g1b[i, 1].astype(F32) + g2b[i].astype(F32)
        a, b = a.astype(BF16), b.astype(BF16)
        stays = at_home & (i == groups - 1)

        @pl.when(stays)
        def _():
            g3[mz // 2, core, :, :qw] = a
            g3[mz // 2, core, :, qw:] = b

        @pl.when(jnp.logical_not(stays))
        def _():
            s3[i, :, :qw] = a
            s3[i, :, qw:] = b
            step3(i).start()

    if groups == 4:
        order = (
            (other_half, 0), (own_half, 0), (other_half, 1), (after0, 0), (rest0, 0), (own_half, 1),
            (other_half, 2), (after0, 1), (rest0, 1), (own_half, 2), (other_half, 3), (after1, 0),
            (after0, 2), (own_half, 3), (after1, 1), (after0, 3), (after2, 0), (rest0, 2),
            (after1, 2), (after2, 1), (rest0, 3), (after1, 3), (after2, 2), (after2, 3),
        )
        for stage, i in order:
            stage(i)
    else:
        def flow(i, carry):
            for stage, lag in ((other_half, 0), (own_half, 0), (after0, 1), (rest0, 1), (after1, 3), (after2, 4)):
                @pl.when((i >= lag) & (i < groups + lag))
                def _():
                    stage(i - lag)

            return carry

        lax.fori_loop(0, groups + 4, flow, 0)

    for q in range(2):
        for w in range(groups // 2):
            mine = at_home & (w == mz // 2) & (q == core)

            @pl.when(jnp.logical_not(mine))
            def _():
                pltpu.make_async_copy(g3.at[w, q], g3.at[w, q], r3.at[w, q]).wait()

        total = g3[0, q].astype(F32)
        for w in range(1, groups // 2):
            total = total + g3[w, q].astype(F32)
        out_ref[:, q * half : (q + 1) * half] = total * scale

    pltpu.make_async_copy(rest, rest, v_send).wait()
    for i in range(1, 4):
        plane_copy(i).wait_send()

    @pl.when(jnp.logical_not(at_home))
    def _():
        home_copy.wait_send()

    for h in range(2):
        @pl.when(jnp.logical_not(at_home))
        def _():
            cond_copy(h, me).wait_send()

        def drain_cond(i, carry):
            cond_copy(h, lax.rem(me + i, n)).wait_send()
            return carry

        lax.fori_loop(1, n, drain_cond, 0)

    def drain_lane(i, carry):
        lane_copy(i).wait_send()
        return carry

    lax.fori_loop(1, ka_size, drain_lane, 0)

    def drain(i, carry):
        for copy in [step0(i)] + step1(i) + step2(i):
            copy.wait_send()

        @pl.when(jnp.logical_not(at_home & (i == groups - 1)))
        def _():
            step3(i).wait_send()

        return carry

    lax.fori_loop(0, groups, drain, 0)


def shards(ka_size, n, cond_orbitals, cond_energy, val_orbitals, val_energy, val_slots, owner_count):
    cond = cond_orbitals[0]
    rows, bc = cond.shape[0], cond.shape[1] // n
    slots = val_slots.shape[2]
    win = 4 * GB
    half = win // 2
    grid = GA * GB
    count = slots * bc
    hcount = count // 2
    groups = n // 4
    nval = ka_size * n
    rb = GB // KG
    table_b = cosine_table(GB)
    table_2 = np.kron(cosine_table(GA), np.eye(rb, dtype=np.float32)).astype(jnp.bfloat16)
    scale = 2.0 / (slots * bc * n)
    vmem = pl.BlockSpec(memory_space=pltpu.VMEM)
    hbm = pl.BlockSpec(memory_space=pl.ANY)
    dma = pltpu.SemaphoreType.DMA
    out = pl.pallas_call(
        functools.partial(kernel, ka_size, n, scale),
        out_shape=pltpu.VMEM((rows, win), F32),
        in_specs=[hbm] * 8,
        out_specs=vmem,
        scratch_shapes=[
            pltpu.SMEM((slots,), jnp.int32),
            pltpu.SMEM((1, 1), jnp.int32),
            pltpu.VMEM((1, bc), F32),
            pltpu.VMEM((1, grid), BF16),
            pltpu.SMEM((1,), BF16),
            pltpu.VMEM((GB, GB), BF16),
            pltpu.VMEM((GA * rb, GA * rb), BF16),
            pltpu.VMEM((rows, n * bc), BF16),
            pltpu.VMEM((2, n, rows // 2, bc), BF16),
            pltpu.VMEM((2, n, rows // 2, bc), BF16),
            pltpu.VMEM((GA + 8, GB), BF16),
            pltpu.VMEM((ka_size, groups, 4, GA + 8, GB), BF16),
            pltpu.VMEM((slots // 2 + 24, bc), F32),
            pltpu.VMEM((slots // 2 + 24, bc), F32),
            pltpu.VMEM((GA, nval, GB), F32),
            pltpu.VMEM((nval, GB), F32),
            pltpu.VMEM((grid, hcount), BF16),
            pltpu.VMEM((8, count), F32),
            pltpu.VMEM((KG, GA * rb, hcount), BF16),
            pltpu.VMEM((grid, count), BF16),
            pltpu.VMEM((win, count), BF16),
            pltpu.VMEM((groups, 4 * rows, half), F32),
            pltpu.VMEM((groups, 4 * rows, half), BF16),
            pltpu.VMEM((groups, 4 * rows, half), BF16),
            *[pltpu.VMEM((groups, 2, rows, half // 2), BF16)] * 4,
            *[pltpu.VMEM((groups, rows, half // 2), BF16)] * 4,
            pltpu.VMEM((groups, rows, half), BF16),
            pltpu.VMEM((groups // 2, 2, rows, half), BF16),
            dma((5,)), dma((2,)), dma(()), dma(()), dma(()), dma(()), dma((4,)), dma((4,)), dma((ka_size,)), dma((ka_size,)), dma(()), dma(()),
            dma((2, n)), dma((2, n)),
            dma((groups,)), dma((groups,)), dma((4, groups)), dma((4, groups)), dma((2, groups)), dma((2, groups)),
            dma((groups,)), dma((groups // 2, 2)),
        ],
        compiler_params=pltpu.CompilerParams(
            collective_id=0, has_side_effects=True, vmem_limit_bytes=60 * 1024 * 1024
        ),
        name="polarizability",
    )(
        val_slots[0, 0], owner_count, cond_energy, val_orbitals, val_energy,
        jnp.asarray(table_b), jnp.asarray(table_2), cond,
    )
    return out[None]


def solution(mesh):
    return jax.shard_map(
        functools.partial(shards, mesh.shape["ka"], mesh.shape["pair"]),
        mesh=mesh,
        in_specs=(
            P("ka", "pair", None),
            P("ka", "pair"),
            P(("ka", "pair"), None),
            P(("ka", "pair")),
            P("ka", "pair", None),
            P("ka", "pair"),
        ),
        out_specs=P("ka", "pair", None),
        check_vma=False,
    )
```

```python
import functools

import jax
import jax.numpy as jnp
import numpy as np
from jax import lax
from jax.experimental import pallas as pl
from jax.experimental.pallas import tpu as pltpu
from jax.sharding import PartitionSpec as P

GA = 16
GB = 128
KG = 8
UNROLL_A = (16, 8)
MESH = pl.DeviceIdType.MESH
F32 = jnp.float32
BF16 = jnp.bfloat16


def cosine_table(length):
    freq = np.arange(length, dtype=np.float32)[:, None]
    point = np.arange(length, dtype=np.float32)[None, :]
    factor = np.where(freq == 0, np.sqrt(np.float32(1.0 / length)), np.sqrt(np.float32(2.0 / length)))
    angle = np.float32(np.pi) * (point + np.float32(0.5)) * freq / np.float32(length)
    return (factor * np.cos(angle)).astype(jnp.bfloat16)


def xor(value, other, limit):
    out, bit = 0, 1
    while bit < limit:
        out = out + lax.rem(value // bit + other // bit, 2) * bit
        bit *= 2
    return out


def kernel(
    ka_size, n, scale,
    slots_hbm, count_hbm, ec_hbm, row_hbm, ev_hbm, tb_hbm, t2_hbm, cond_hbm,
    out_ref,
    slots_ref, count_ref, ec_ref, row_ref, ev_ref, tb, t2, cond, csend, cblk, vmsg, vals, hmsg, hrecv, allv, evm, mult, wrow, first, moved, wt,
    own, p0s, p0r, s1a, s1b, g1a, g1b, s2a, s2b, g2a, g2b, s3, g3,
    e_sem, t_sem, k_sem, v_own, v_send, v_recv, p_send, p_recv, l_send, l_recv, h_send, h_recv, c_send, c_recv,
    q0, r0, q1, r1, q2, r2, q3, r3,
):
    my_ka = lax.axis_index("ka")
    me = lax.axis_index("pair")
    core = lax.rem(my_ka, 2)
    kb = my_ka - core
    mz = me // 4
    xy = lax.rem(me, 4)
    zbit = lax.rem(mz, 2)
    sibling = kb + 1 - core
    slots = slots_ref.shape[0]
    bc = ec_ref.shape[1]
    hb = bc // 2
    pairs = slots // 2
    count = slots * bc
    hcount = count // 2
    rows = cond.shape[0]
    hr = rows // 2
    win = out_ref.shape[1]
    half = win // 2
    qw = half // 2
    groups = n // 4
    per_a = n // GA
    rb = GB // KG
    nval = ka_size * n
    home_owner = me + 4 * (core - zbit)
    at_home = core == zbit

    def remote(src, dst, ssem, rsem, ka, pair):
        return pltpu.make_async_remote_copy(
            src_ref=src, dst_ref=dst, send_sem=ssem, recv_sem=rsem,
            device_id=(ka, pair), device_id_type=MESH,
        )

    barrier = pltpu.get_barrier_semaphore()

    def greet(i, carry):
        other = lax.rem(me + i, n)
        for k in (my_ka, sibling):
            pl.semaphore_signal(barrier, inc=1, device_id=(k, other), device_id_type=MESH)
        return carry

    def greet_core(i, carry):
        pl.semaphore_signal(
            barrier, inc=1, device_id=(lax.rem(kb + i, ka_size), me), device_id_type=MESH
        )
        return carry

    cond_in = pltpu.make_async_copy(cond_hbm, cond, k_sem)
    lax.fori_loop(1, n, greet, 0)
    pl.semaphore_signal(barrier, inc=1, device_id=(sibling, me), device_id_type=MESH)
    lax.fori_loop(2, ka_size, greet_core, 0)
    small = [
        pltpu.make_async_copy(src, dst, e_sem.at[i])
        for i, (src, dst) in enumerate((
            (slots_hbm, slots_ref), (count_hbm, count_ref), (ec_hbm, ec_ref), (row_hbm, row_ref), (ev_hbm, ev_ref),
        ))
    ]
    for copy in small:
        copy.start()
    cond_in.start()
    tables = (pltpu.make_async_copy(tb_hbm, tb, t_sem.at[0]), pltpu.make_async_copy(t2_hbm, t2, t_sem.at[1]))
    for copy in tables:
        copy.start()

    for copy in small:
        copy.wait()

    row = row_ref[...].astype(F32)
    grid_rows = [row[:, a * GB : (a + 1) * GB] for a in range(GA)]
    energy = jnp.broadcast_to(ev_ref[0].astype(F32), (8, GB))
    vmsg[...] = jnp.concatenate(grid_rows + [energy], axis=0).astype(BF16)
    own_val = pltpu.make_async_copy(vmsg, vals.at[my_ka, mz, xy], v_own)
    own_val.start()

    low = lax.broadcasted_iota(jnp.int32, (8, bc), 1) < hb
    low1 = lax.broadcasted_iota(jnp.int32, (1, bc), 1) < hb
    for t in range(pairs):
        hmsg[t : t + 1] = jnp.where(low1, slots_ref[2 * t], slots_ref[2 * t + 1]).astype(F32)
    ec = jnp.broadcast_to(ec_ref[...], (8, bc))
    turned = pltpu.roll(ec, hb, 1)
    hmsg[pairs : pairs + 8] = jnp.where(low, ec, turned)
    hmsg[pairs + 8 : pairs + 16] = jnp.where(low, turned, ec)
    hmsg[pairs + 16 : pairs + 24] = jnp.broadcast_to(count_ref[0, 0], (8, bc)).astype(F32)

    cond_in.wait()
    low_c = lax.broadcasted_iota(jnp.int32, (hr, bc), 1) < hb

    def pack(o, carry):
        block = cond[:, pl.ds(pl.multiple_of(o * bc, bc), bc)].astype(F32)
        top, bot = block[:hr], block[hr:]
        csend[0, o] = jnp.where(low_c, top, pltpu.roll(bot, hb, 1)).astype(BF16)
        csend[1, o] = jnp.where(low_c, pltpu.roll(top, hb, 1), bot).astype(BF16)
        return carry

    lax.fori_loop(0, n, pack, 0, unroll=4)
    own_val.wait()

    pl.semaphore_wait(barrier, 2 * n - 1 + ka_size - 2)

    def send_val(i, carry):
        remote(
            vmsg, vals.at[my_ka, mz, xy], v_send, v_recv, my_ka, lax.rem(mz + i, groups) * 4 + xy
        ).start()
        return carry

    lax.fori_loop(1, groups, send_val, 0)
    column = vals.at[my_ka, pl.ds(0, groups), xy]
    rest = vals.at[my_ka, pl.ds(0, groups - 1), xy]

    def plane_copy(i):
        return remote(column, column, p_send.at[i], p_recv.at[i], my_ka, mz * 4 + xor(xy, i, 4))

    home_copy = remote(hmsg, hrecv, h_send, h_recv, sibling, home_owner)

    @pl.when(at_home)
    def _():
        hrecv[...] = hmsg[...]

    @pl.when(jnp.logical_not(at_home))
    def _():
        home_copy.start()

    def cond_copy(h, o):
        obit = lax.rem(o // 4, 2)
        return remote(
            csend.at[h, o], cblk.at[h, me], c_send.at[h, o], c_recv.at[h, me],
            kb + obit, o + 4 * (core - obit),
        )

    def own_cond(h):
        return pltpu.make_async_copy(csend.at[h, me], cblk.at[h, me], c_recv.at[h, me])

    def send_low(h):
        @pl.when(at_home)
        def _():
            own_cond(h).start()

        @pl.when(jnp.logical_not(at_home))
        def _():
            cond_copy(h, me).start()

        lax.fori_loop(1, n // 2, functools.partial(send_cond, h), 0)

    def send_cond(h, i, carry):
        cond_copy(h, lax.rem(me + i, n)).start()
        return carry

    def send_high(h):
        lax.fori_loop(n // 2, n, functools.partial(send_cond, h), 0)

    send_low(0)
    send_high(0)
    pltpu.make_async_copy(rest, rest, v_recv).wait()
    for i in range(1, 4):
        plane_copy(i).start()
    send_low(1)
    for i in range(1, 4):
        peer = vals.at[my_ka, pl.ds(0, groups), xor(xy, i, 4)]
        pltpu.make_async_copy(peer, peer, p_recv.at[i]).wait()

    def lane_copy(i):
        other = lax.rem(my_ka + i, ka_size)
        return remote(vals.at[my_ka], vals.at[my_ka], l_send.at[other], l_recv.at[my_ka], other, me)

    def send_lane(i, carry):
        lane_copy(i).start()
        return carry

    def wait_lane(i, carry):
        other = lax.rem(my_ka + i, ka_size)
        pltpu.make_async_copy(vals.at[other], vals.at[other], l_recv.at[other]).wait()
        return carry

    lax.fori_loop(1, ka_size, send_lane, 0)
    lax.fori_loop(1, ka_size, wait_lane, 0)
    send_high(1)

    @pl.when(jnp.logical_not(at_home))
    def _():
        home_copy.wait_recv()

    def unfold(v, carry):
        tile = vals[v // n, lax.rem(v, n) // 4, lax.rem(v, 4)].astype(F32)
        allv[:, pl.ds(v, 1), :] = tile[:GA][:, None, :]
        evm[pl.ds(v, 1), :] = tile[GA : GA + 1]
        return carry

    lax.fori_loop(0, nval, unfold, 0, unroll=8)
    index = lax.broadcasted_iota(jnp.int32, (nval, bc), 0).astype(F32)
    hot = []
    for t in range(pairs):
        one = jnp.where(index == hrecv[t : t + 1], 1.0, 0.0)
        hot.append(one.astype(BF16))
        e_v = jnp.sum(one * evm[...], axis=0, keepdims=True)
        slot = jnp.where(low1, 2.0 * t, 2.0 * t + 1.0)
        live = jnp.where(slot < hrecv[pairs + 16 : pairs + 17], 1.0, 0.0)
        for h in range(2):
            e_c = hrecv[pairs + 8 * h : pairs + 8 * h + 1]
            wrow[0:1, h * hcount + t * bc : h * hcount + (t + 1) * bc] = live * 2.0 / (e_c - e_v)
    hot = jnp.concatenate(hot, axis=1)

    def spread(a, carry):
        mult[pl.ds(pl.multiple_of(a * GB, GB), GB), :] = lax.dot_general(
            allv[a].astype(BF16), hot, (((0,), (0,)), ((), ())), preferred_element_type=F32
        ).astype(BF16)
        return carry

    lax.fori_loop(0, GA, spread, 0, unroll=8)

    for copy in tables:
        copy.wait()
    home_a = home_owner // per_a
    wide = min(2 * bc, hcount)

    for h in range(2):
        def do_first(step, carry):
            blocks = [
                lax.rem(home_a + GA - step * UNROLL_A[h] - r, GA) for r in range(UNROLL_A[h])
            ]
            for a in blocks:
                for q in range(per_a):
                    src = a * per_a + q
                    pltpu.make_async_copy(cblk.at[h, src], cblk.at[h, src], c_recv.at[h, src]).wait()
            for a in blocks:
                tops, bots = [], []
                for q in range(per_a):
                    part = cblk[h, a * per_a + q].astype(F32)
                    turn = pltpu.roll(part, hb, 1)
                    tops.append(jnp.where(low_c, part, turn))
                    tops.append(jnp.where(low_c, turn, part))
                block = jnp.concatenate(tops, axis=0).astype(BF16)
                block = jnp.concatenate([block] * (wide // bc), axis=1)
                for at in range(0, hcount, wide):
                    x = block * mult[pl.ds(pl.multiple_of(a * GB, GB), GB), at : at + wide]
                    f = jnp.dot(tb[...], x, preferred_element_type=F32).astype(BF16)
                    first[:, pl.ds(pl.multiple_of(a * rb, rb), rb), at : at + wide] = f.reshape(KG, rb, wide)
            return carry

        lax.fori_loop(0, GA // UNROLL_A[h], do_first, 0)

        def do_moved(kg, carry):
            start = pl.multiple_of(kg * rb, rb)
            for at in range(0, hcount, wide):
                sl = slice(h * hcount + at, h * hcount + at + wide)
                mv = jnp.dot(t2[...], first[kg, :, at : at + wide], preferred_element_type=F32).astype(BF16)
                for j in range(GA):
                    piece = mv[j * rb : (j + 1) * rb]
                    moved[pl.ds(j * GB + start, rb), sl] = piece
                    if j * GB < win:
                        wt[pl.ds(j * GB + start, rb), sl] = (piece.astype(F32) * wrow[0:1, sl]).astype(BF16)
            return carry

        lax.fori_loop(0, KG, do_moved, 0, unroll=True)

    mx, my = lax.rem(me, 2), lax.rem(me, 4) // 2
    px, py = 1 - mx, 1 - my
    x_peer = mz * 4 + my * 2 + px
    y_peer = mz * 4 + py * 2 + mx

    def target(i):
        step = groups - 1 - i
        if groups == 4 and step >= 2:
            step = 5 - step
        return xor(mz, step, groups)

    def step0(i):
        return remote(p0s.at[i], p0r.at[i], q0.at[i], r0.at[i], sibling, me)

    def step1(i):
        return [
            remote(s1a.at[i, 0], g1a.at[i, 0], q1.at[0, i], r1.at[0, i], my_ka, x_peer),
            remote(s1b.at[i, 0], g1b.at[i, 0], q1.at[1, i], r1.at[1, i], my_ka, y_peer),
            remote(s1a.at[i, 1], g1a.at[i, 1], q1.at[2, i], r1.at[2, i], my_ka, x_peer),
            remote(s1b.at[i, 1], g1b.at[i, 1], q1.at[3, i], r1.at[3, i], my_ka, y_peer),
        ]

    def step2(i):
        return [
            remote(s2a.at[i], g2a.at[i], q2.at[0, i], r2.at[0, i], my_ka, y_peer),
            remote(s2b.at[i], g2b.at[i], q2.at[1, i], r2.at[1, i], my_ka, x_peer),
        ]

    def step3(i, part):
        return remote(
            s3.at[i, part], g3.at[mz // 2, core, part], q3.at[i, part], r3.at[mz // 2, core, part],
            kb + zbit, target(i) * 4 + xy,
        )

    def product(i, side):
        z = target(i)
        return lax.dot_general(
            moved[pl.ds(pl.multiple_of(z * 4 * rows, 4 * rows), 4 * rows), :],
            wt[pl.ds(pl.multiple_of(side * half, half), half), :],
            (((1,), (1,)), ((), ())), preferred_element_type=F32,
        )

    def pair_sum(i, y, x, b):
        at = pl.ds(pl.multiple_of((2 * y + x) * rows, rows), rows)
        sl = slice(b * qw, (b + 1) * qw)
        return own[i, at, sl] + p0r[i, at, sl].astype(F32)

    def other_half(i):
        p0s[i] = product(i, 1 - core).astype(BF16)
        step0(i).start()

    def own_half(i):
        own[i] = product(i, core)

    def after0(i):
        step0(i).wait_recv()
        copies = step1(i)
        s1a[i, 0] = pair_sum(i, py, px, 0).astype(BF16)
        copies[0].start()
        s1b[i, 0] = pair_sum(i, py, px, 1).astype(BF16)
        copies[1].start()

    def rest0(i):
        copies = step1(i)
        s1a[i, 1] = pair_sum(i, my, px, 0).astype(BF16)
        copies[2].start()
        s1b[i, 1] = pair_sum(i, py, mx, 1).astype(BF16)
        copies[3].start()

    def after1(i):
        first_copies, copies = step1(i), step2(i)
        first_copies[0].wait_recv()
        s2a[i] = (pair_sum(i, py, mx, 0) + g1a[i, 0].astype(F32)).astype(BF16)
        copies[0].start()
        first_copies[1].wait_recv()
        s2b[i] = (pair_sum(i, my, px, 1) + g1b[i, 0].astype(F32)).astype(BF16)
        copies[1].start()

    def after2(i):
        first_copies, second_copies = step1(i), step2(i)
        stays = at_home & (i == groups - 1)
        for part, (g1, g2) in enumerate(((g1a, g2a), (g1b, g2b))):
            first_copies[2 + part].wait_recv()
            second_copies[part].wait_recv()
            total = (pair_sum(i, my, mx, part) + g1[i, 1].astype(F32) + g2[i].astype(F32)).astype(BF16)

            @pl.when(stays)
            def _():
                g3[mz // 2, core, part] = total

            @pl.when(jnp.logical_not(stays))
            def _():
                s3[i, part] = total
                step3(i, part).start()

    if groups == 4:
        order = (
            (other_half, 0), (own_half, 0), (other_half, 1), (after0, 0), (rest0, 0), (own_half, 1),
            (other_half, 2), (after0, 1), (rest0, 1), (own_half, 2), (other_half, 3), (after1, 0),
            (after0, 2), (own_half, 3), (after1, 1), (after0, 3), (after2, 0), (rest0, 2),
            (after1, 2), (after2, 1), (rest0, 3), (after1, 3), (after2, 2), (after2, 3),
        )
        for stage, i in order:
            stage(i)
    else:
        def flow(i, carry):
            for stage, lag in ((other_half, 0), (own_half, 0), (after0, 1), (rest0, 1), (after1, 3), (after2, 4)):
                @pl.when((i >= lag) & (i < groups + lag))
                def _():
                    stage(i - lag)

            return carry

        lax.fori_loop(0, groups + 4, flow, 0)

    for q in range(2):
        for part in range(2):
            total = None
            for w in range(groups // 2):
                mine = at_home & (w == mz // 2) & (q == core)

                @pl.when(jnp.logical_not(mine))
                def _():
                    pltpu.make_async_copy(g3.at[w, q, part], g3.at[w, q, part], r3.at[w, q, part]).wait()

                piece = g3[w, q, part].astype(F32)
                total = piece if total is None else total + piece
            out_ref[:, q * half + part * qw : q * half + (part + 1) * qw] = total * scale

    pltpu.make_async_copy(rest, rest, v_send).wait()
    for i in range(1, 4):
        plane_copy(i).wait_send()

    @pl.when(jnp.logical_not(at_home))
    def _():
        home_copy.wait_send()

    for h in range(2):
        @pl.when(jnp.logical_not(at_home))
        def _():
            cond_copy(h, me).wait_send()

        def drain_cond(i, carry):
            cond_copy(h, lax.rem(me + i, n)).wait_send()
            return carry

        lax.fori_loop(1, n, drain_cond, 0)

    def drain_lane(i, carry):
        lane_copy(i).wait_send()
        return carry

    lax.fori_loop(1, ka_size, drain_lane, 0)

    for i in range(groups):
        for copy in [step0(i)] + step1(i) + step2(i):
            copy.wait_send()

        @pl.when(jnp.logical_not(at_home & (i == groups - 1)))
        def _():
            for part in range(2):
                step3(i, part).wait_send()


def shards(ka_size, n, cond_orbitals, cond_energy, val_orbitals, val_energy, val_slots, owner_count):
    cond = cond_orbitals[0]
    rows, bc = cond.shape[0], cond.shape[1] // n
    slots = val_slots.shape[2]
    win = 4 * GB
    half = win // 2
    grid = GA * GB
    count = slots * bc
    hcount = count // 2
    groups = n // 4
    nval = ka_size * n
    rb = GB // KG
    table_b = cosine_table(GB)
    table_2 = np.kron(cosine_table(GA), np.eye(rb, dtype=np.float32)).astype(jnp.bfloat16)
    scale = 2.0 / (slots * bc * n)
    vmem = pl.BlockSpec(memory_space=pltpu.VMEM)
    hbm = pl.BlockSpec(memory_space=pl.ANY)
    dma = pltpu.SemaphoreType.DMA
    out = pl.pallas_call(
        functools.partial(kernel, ka_size, n, scale),
        out_shape=pltpu.VMEM((rows, win), F32),
        in_specs=[hbm] * 8,
        out_specs=vmem,
        scratch_shapes=[
            pltpu.SMEM((slots,), jnp.int32),
            pltpu.SMEM((1, 1), jnp.int32),
            pltpu.VMEM((1, bc), F32),
            pltpu.VMEM((1, grid), BF16),
            pltpu.SMEM((1,), BF16),
            pltpu.VMEM((GB, GB), BF16),
            pltpu.VMEM((GA * rb, GA * rb), BF16),
            pltpu.VMEM((rows, n * bc), BF16),
            pltpu.VMEM((2, n, rows // 2, bc), BF16),
            pltpu.VMEM((2, n, rows // 2, bc), BF16),
            pltpu.VMEM((GA + 8, GB), BF16),
            pltpu.VMEM((ka_size, groups, 4, GA + 8, GB), BF16),
            pltpu.VMEM((slots // 2 + 24, bc), F32),
            pltpu.VMEM((slots // 2 + 24, bc), F32),
            pltpu.VMEM((GA, nval, GB), F32),
            pltpu.VMEM((nval, GB), F32),
            pltpu.VMEM((grid, hcount), BF16),
            pltpu.VMEM((8, count), F32),
            pltpu.VMEM((KG, GA * rb, hcount), BF16),
            pltpu.VMEM((grid, count), BF16),
            pltpu.VMEM((win, count), BF16),
            pltpu.VMEM((groups, 4 * rows, half), F32),
            pltpu.VMEM((groups, 4 * rows, half), BF16),
            pltpu.VMEM((groups, 4 * rows, half), BF16),
            *[pltpu.VMEM((groups, 2, rows, half // 2), BF16)] * 4,
            *[pltpu.VMEM((groups, rows, half // 2), BF16)] * 4,
            pltpu.VMEM((groups, 2, rows, half // 2), BF16),
            pltpu.VMEM((groups // 2, 2, 2, rows, half // 2), BF16),
            dma((5,)), dma((2,)), dma(()), dma(()), dma(()), dma(()), dma((4,)), dma((4,)), dma((ka_size,)), dma((ka_size,)), dma(()), dma(()),
            dma((2, n)), dma((2, n)),
            dma((groups,)), dma((groups,)), dma((4, groups)), dma((4, groups)), dma((2, groups)), dma((2, groups)),
            dma((groups, 2)), dma((groups // 2, 2, 2)),
        ],
        compiler_params=pltpu.CompilerParams(
            collective_id=0, has_side_effects=True, vmem_limit_bytes=60 * 1024 * 1024
        ),
        name="polarizability",
    )(
        val_slots[0, 0], owner_count, cond_energy, val_orbitals, val_energy,
        jnp.asarray(table_b), jnp.asarray(table_2), cond,
    )
    return out[None]


def solution(mesh):
    return jax.shard_map(
        functools.partial(shards, mesh.shape["ka"], mesh.shape["pair"]),
        mesh=mesh,
        in_specs=(
            P("ka", "pair", None),
            P("ka", "pair"),
            P(("ka", "pair"), None),
            P(("ka", "pair")),
            P("ka", "pair", None),
            P("ka", "pair"),
        ),
        out_specs=P("ka", "pair", None),
        check_vma=False,
    )
```
